32 devices in a mesh: groups: 2 (over x), ty: 4 (over y, core), tx: 4 (over z).
Axes of the slice: x: 2, y: 2, z: 4, core: 2. Of those that a mesh axis runs over, the one named last changes fastest.
Arguments:
- object_planes: float32 [4, 2048, 1024], P(None, ('groups', 'ty'), 'tx'), parts along dimension 1, may hold values from -5 to 5
- probe: float32 [2, 256, 256], replicated, may hold values from -5 to 5
- phase: float32 [256, 256], replicated, may hold values from -3.140625 to 3.140625
- coords: int32 [8, 4, 4, 2], P(('groups', 'ty'), 'tx'), parts along dimension 0, may hold values from 0 to 255
- live: int32 [8, 4], P(('groups', 'ty'), 'tx'), parts along dimension 0, may hold values from 0 to 4, as said below
- amplitude: float32 [8, 4, 4, 256, 256], P(('groups', 'ty'), 'tx'), parts along dimension 0, may hold values from 0 to 2
Outputs:
- updated: float32 [4, 2048, 1024], P(None, ('groups', 'ty'), 'tx'), parts along dimension 1
The draws below stay inside these ranges and needn't reach their ends.
There are 2 independent parts, one for each index of `groups`. The reference program is written for one: setup_inputs(seed, part) draws one part's arguments, and reference() takes and returns one part's arrays. A program takes and returns all parts, laid end to end along the dimension named above; an argument that names none is the same for every part. Nothing has to cross between parts.
Inputs may be any that keep to these rules, and one draw needn't show every extreme that they name: Only slots below live of their tile are used; some tile holds 4 live slots.
All inputs are finite; a program needn't handle non-finite values.
Results may differ from the reference program's by a relative error of at most 0.0003.
Values sent between devices are 32-bit elements; how exact they have to be, the bound alone decides.
A program may use at most 128 MiB of HBM per device.

```python
import math
import jax
import jax.numpy as jnp
from jax import lax

W = 256
SLOTS = 4
TILES_Y = 4
TILES_X = 4
NH = 1024
NW = 1024


def draw_live(key, part):
    key_base, key_cols, key_start = jax.random.split(key, 3)
    base_load = jax.random.randint(key_base, (TILES_Y, TILES_X), 0, 3)
    dense_cols = jax.random.randint(key_cols, (2,), 0, TILES_X)
    start_row = jax.random.randint(key_start, (), 0, TILES_Y)
    row_hit = (jnp.arange(TILES_Y) - start_row) % TILES_Y < max(TILES_Y // 4, 1)
    col_hit = jnp.any(jnp.arange(TILES_X)[None, :] == dense_cols[:, None], axis=0)
    dense = row_hit[:, None] & col_hit[None, :]
    return jnp.where(dense, SLOTS, base_load).astype(jnp.int32)


def touch_ends(array, key, smallest, high):
    longest = array.shape.index(max(array.shape))
    spots = []
    for shift in (0, 1):
        where = [jax.random.randint(jax.random.fold_in(key, axis), (), 0, length) for axis, length in enumerate(array.shape)]
        where[longest] = (where[longest] + shift) % array.shape[longest]
        spots.append(tuple(where))
    return array.at[spots[0]].set(smallest).at[spots[1]].set(high)


def level_of(key, dims, shards, smallest, top_value):
    def one(axis_at, blocks):
        draws = jax.random.uniform(jax.random.fold_in(jax.random.fold_in(key, 6), axis_at), (blocks,), jnp.float32, smallest / len(shards), top_value / len(shards))
        return jnp.repeat(jnp.exp(draws), dims[axis_at] // blocks).reshape((-1,) + (1,) * (len(dims) - axis_at - 1))

    gain = one(*shards[0])
    for cut in shards[1:]:
        gain = gain * one(*cut)
    return gain


def noise(rng, shape, deviation, bound, pieces=(), kind=jnp.bfloat16):
    loudness = level_of(rng, shape, pieces, -0.22, 0.18) if pieces else 1.0
    values = jax.random.normal(rng, shape, jnp.float32) * deviation * loudness
    return jnp.minimum(jnp.maximum(values, -bound), bound).astype(kind)


def setup_inputs(seed: int = 0, part: int = 0) -> dict:
    seeds = jax.random.split(jax.random.key(seed), 7)
    part_keys = jax.random.split(jax.random.fold_in(seeds[6], part), 7)
    return {
        "object_planes": noise(part_keys[0], (4, NH, NW), 0.7, 5.0, ((1, 4), (2, 4)), jnp.float32),
        "probe": noise(seeds[1], (2, W, W), 0.7, 5.0, (), jnp.float32),
        "phase": jnp.clip(jax.random.uniform(seeds[2], (W, W), jnp.float32, -3.140625, 3.140625), -3.140625, 3.140625),
        "coords": touch_ends(jax.random.randint(part_keys[3], (TILES_Y, TILES_X, SLOTS, 2), 0, W), jax.random.fold_in(part_keys[3], 1), 0, W - 1).astype(jnp.int32),
        "live": draw_live(jax.random.fold_in(jax.random.fold_in(seeds[6], part), 71), part),
        "amplitude": jnp.clip(2.0 * jax.random.uniform(part_keys[5], (TILES_Y, TILES_X, SLOTS, W, W), jnp.float32) ** level_of(part_keys[5], (TILES_Y, TILES_X, SLOTS, W, W), ((0, 4), (1, 4)), -0.2, 0.2), 0.0, 2.0),
    }


HIGH = lax.Precision.HIGHEST

def dft_tables(probe_width):
    index_grid = jnp.arange(probe_width, dtype=jnp.int32)[:, None] * jnp.arange(probe_width, dtype=jnp.int32)[None, :] % probe_width
    angles = index_grid.astype(jnp.float32) * (2.0 * math.pi / probe_width)
    norm_scale = 1.0 / math.sqrt(probe_width)
    return (jnp.cos(angles) * norm_scale, -jnp.sin(angles) * norm_scale)

def product(left_mat, right_mat):
    return jnp.dot(left_mat, right_mat, precision=HIGH, preferred_element_type=jnp.float32)

def transform(real_part, imag_part, cos_table, sin_table):
    left_r = product(cos_table, real_part) - product(sin_table, imag_part)
    left_i = product(cos_table, imag_part) + product(sin_table, real_part)
    out_r = product(left_r, cos_table) - product(left_i, sin_table)
    out_i = product(left_r, sin_table) + product(left_i, cos_table)
    return (out_r, out_i)

def slot_terms(probe, phase_r, phase_i, cos_table, sin_table, patch, amp_plane):
    probe_r, probe_i = (probe[0], probe[1])
    first_r, first_i, second_r, second_i = (patch[0], patch[1], patch[2], patch[3])
    wave_one_r = probe_r * first_r - probe_i * first_i
    wave_one_i = probe_r * first_i + probe_i * first_r
    spec_r, spec_i = transform(wave_one_r, wave_one_i, cos_table, sin_table)
    moved_r = spec_r * phase_r - spec_i * phase_i
    moved_i = spec_r * phase_i + spec_i * phase_r
    wave_two_r, wave_two_i = transform(moved_r, moved_i, cos_table, -sin_table)
    exit_r = wave_two_r * second_r - wave_two_i * second_i
    exit_i = wave_two_r * second_i + wave_two_i * second_r
    far_r, far_i = transform(exit_r, exit_i, cos_table, sin_table)
    ratio = amp_plane / jnp.maximum(jnp.sqrt(far_r * far_r + far_i * far_i), 0.5) - 1.0
    back_r, back_i = transform(far_r * ratio, far_i * ratio, cos_table, -sin_table)
    grad_two_r = wave_two_r * back_r + wave_two_i * back_i
    grad_two_i = wave_two_r * back_i - wave_two_i * back_r
    inner_r = second_r * back_r + second_i * back_i
    inner_i = second_r * back_i - second_i * back_r
    turn_r, turn_i = transform(inner_r, inner_i, cos_table, sin_table)
    undo_r = turn_r * phase_r + turn_i * phase_i
    undo_i = turn_i * phase_r - turn_r * phase_i
    prior_r, prior_i = transform(undo_r, undo_i, cos_table, -sin_table)
    grad_one_r = probe_r * prior_r + probe_i * prior_i
    grad_one_i = probe_r * prior_i - probe_i * prior_r
    power_two = wave_two_r * wave_two_r + wave_two_i * wave_two_i
    return jnp.stack([grad_one_r, grad_one_i, grad_two_r, grad_two_i, power_two])

def reference(object_planes, probe, phase, coords, live, amplitude):
    probe_width = probe.shape[-1]
    cos_table, sin_table = dft_tables(probe_width)
    phase_r, phase_i = (jnp.cos(phase), jnp.sin(phase))
    padded = jnp.pad(object_planes, ((0, 0), (0, probe_width), (0, probe_width)))
    totals = jnp.zeros((6,) + padded.shape[1:], jnp.float32)
    probe_power = probe[0] * probe[0] + probe[1] * probe[1]
    tiles_rows, tiles_cols, slot_count = (coords.shape[0], coords.shape[1], coords.shape[2])
    flat_coords = coords.reshape(-1, 2)
    flat_amp = amplitude.reshape(-1, probe_width, probe_width)
    tile_row = jnp.repeat(jnp.arange(tiles_rows, dtype=jnp.int32), tiles_cols * slot_count)
    tile_col = jnp.tile(jnp.repeat(jnp.arange(tiles_cols, dtype=jnp.int32), slot_count), tiles_rows)
    slot_ids = jnp.tile(jnp.arange(slot_count, dtype=jnp.int32), tiles_rows * tiles_cols)
    active = slot_ids < live.reshape(-1)[tile_row * tiles_cols + tile_col]

    def accumulate(totals, slot_data):
        where_yx, amp_plane, row_tile, col_tile, is_live = slot_data
        top_row = (row_tile * probe_width + where_yx[0]).astype(jnp.int32)
        left_col = (col_tile * probe_width + where_yx[1]).astype(jnp.int32)
        zero_index = jnp.int32(0)
        patch = lax.dynamic_slice(padded, (zero_index, top_row, left_col), (4, probe_width, probe_width))

        def compute():
            gradients = slot_terms(probe, phase_r, phase_i, cos_table, sin_table, patch, amp_plane)
            return jnp.concatenate([gradients[0:2], probe_power[None], gradients[2:5]])

        def skip():
            return jnp.zeros((6, probe_width, probe_width), jnp.float32)
        contrib = lax.cond(is_live, compute, skip)
        current = lax.dynamic_slice(totals, (zero_index, top_row, left_col), (6, probe_width, probe_width))
        return (lax.dynamic_update_slice(totals, current + contrib, (zero_index, top_row, left_col)), None)
    totals, _ = lax.scan(accumulate, totals, (flat_coords, flat_amp, tile_row, tile_col, active))
    totals = totals[:, :object_planes.shape[1], :object_planes.shape[2]]
    first = object_planes[0:2] + totals[0:2] / (totals[2:3] + 1.0)
    second = object_planes[2:4] + totals[3:5] / (totals[5:6] + 1.0)
    return jnp.concatenate([first, second])
```

```python
import math

import jax
import jax.numpy as jnp
import numpy as np
from jax import lax
from jax.experimental import pallas as pl
from jax.experimental.pallas import tpu as pltpu
from jax.sharding import PartitionSpec as P

F32 = jnp.float32
BF16 = jnp.bfloat16
CHUNKS = 2


def dft_tables(width):
    half = width // 2
    scale = 1.0 / math.sqrt(width)

    def stacked(table, axis):
        table = table.astype(np.float32)
        high = table.astype(BF16)
        low = (table - high.astype(np.float32)).astype(BF16)
        return np.concatenate([high, high, low], axis=axis)

    lefts, rights = [], []
    for parity in range(2):
        index = (2 * np.arange(half) + parity)[:, None] * np.arange(half)[None, :] % width
        angles = index * (2.0 * math.pi / width)
        real, imag = np.cos(angles) * scale, -np.sin(angles) * scale
        whole = np.block([[real, -imag], [imag, real]])
        lefts.append((stacked(whole, 1), stacked(whole.T, 1)))
        rights.append((stacked(whole.T, 0), stacked(whole, 0)))
    left = np.stack([lefts[parity][way] for way in range(2) for parity in range(2)])
    right = np.stack([rights[parity][way] for way in range(2) for parity in range(2)])
    return jnp.asarray(left), jnp.asarray(right)


def split(value):
    high = value.astype(BF16)
    low = (value - high.astype(F32)).astype(BF16)
    return high, low


def tripled(value, axis):
    high, low = split(value)
    return jnp.concatenate([high, low, high], axis=axis)


def to_spectrum(values, left, right):
    width = values[0][0].shape[0]
    half = width // 2
    sides = []
    for parity in range(2):
        columns = []
        for pair in values:
            parts = [v[:half] - v[half:] if parity else v[:half] + v[half:] for v in pair]
            columns.append(tripled(jnp.concatenate(parts, axis=0), 0))
        data = jnp.concatenate(columns, axis=1)
        sides.append(jnp.dot(left[parity][...], data, preferred_element_type=F32))
    outs = []
    for parity in range(2):
        rows = []
        for at in range(len(values)):
            cut = slice(at * width, (at + 1) * width)
            parts = []
            for part in (slice(0, half), slice(half, width)):
                v = jnp.concatenate([sides[0][part, cut], sides[1][part, cut]], axis=0)
                parts.append(v[:, :half] - v[:, half:] if parity else v[:, :half] + v[:, half:])
            rows.append(tripled(jnp.concatenate(parts, axis=1), 1))
        data = jnp.concatenate(rows, axis=0)
        outs.append(jnp.dot(data, right[parity][...], preferred_element_type=F32))
    result = []
    for at in range(len(values)):
        rows = slice(at * width, (at + 1) * width)
        real = jnp.concatenate([outs[0][rows, :half], outs[1][rows, :half]], axis=1)
        imag = jnp.concatenate([outs[0][rows, half:], outs[1][rows, half:]], axis=1)
        result.append((real, imag))
    return result


def from_spectrum(values, left, right):
    width = values[0][0].shape[0]
    half = width // 2
    halves = (slice(0, half), slice(half, width))
    sides = []
    for parity in range(2):
        columns = []
        for pair in values:
            parts = [v[halves[parity]] for v in pair]
            columns.append(tripled(jnp.concatenate(parts, axis=0), 0))
        data = jnp.concatenate(columns, axis=1)
        sides.append(jnp.dot(left[parity][...], data, preferred_element_type=F32))
    tops = sides[0] + sides[1]
    lows = sides[0] - sides[1]
    outs = []
    for parity in range(2):
        rows = []
        for at in range(len(values)):
            cut = slice(at * width + parity * half, at * width + (parity + 1) * half)
            parts = [
                jnp.concatenate([tops[part, cut], lows[part, cut]], axis=0) for part in halves
            ]
            rows.append(tripled(jnp.concatenate(parts, axis=1), 1))
        data = jnp.concatenate(rows, axis=0)
        outs.append(jnp.dot(data, right[parity][...], preferred_element_type=F32))
    total, gap = outs[0] + outs[1], outs[0] - outs[1]
    result = []
    for at in range(len(values)):
        rows = slice(at * width, (at + 1) * width)
        real = jnp.concatenate([total[rows, :half], gap[rows, :half]], axis=1)
        imag = jnp.concatenate([total[rows, half:], gap[rows, half:]], axis=1)
        result.append((real, imag))
    return result


def neighbours():
    row, column = lax.axis_index("ty"), lax.axis_index("tx")
    has = {
        "up": row > 0,
        "down": row < lax.axis_size("ty") - 1,
        "left": column > 0,
        "right": column < lax.axis_size("tx") - 1,
    }
    where = {
        "up": {"ty": row - 1},
        "down": {"ty": row + 1},
        "left": {"tx": column - 1},
        "right": {"tx": column + 1},
    }
    return has, where


def greet(has, where):
    barrier = pltpu.get_barrier_semaphore()
    for side, there in has.items():

        @pl.when(there)
        def _():
            pl.semaphore_signal(
                barrier, inc=1, device_id=where[side], device_id_type=pl.DeviceIdType.MESH
            )

    peers = sum(there.astype(jnp.int32) for there in has.values())
    pl.semaphore_wait(barrier, peers)


class Links:
    def __init__(self, sems):
        self.sems, self.every = sems, []

    def link(self, source, target, device, sends, receives):
        at = len(self.every)
        made = Link(source, target, self.sems, at, device, sends, receives)
        self.every.append(made)
        return made

    def sent(self):
        for made in self.every:
            made.sent()


class Link:
    def __init__(self, source, target, sems, at, device, sends, receives):
        self.copy = pltpu.make_async_remote_copy(
            src_ref=source,
            dst_ref=target,
            send_sem=sems[0].at[at],
            recv_sem=sems[1].at[at],
            device_id=device,
            device_id_type=pl.DeviceIdType.MESH,
        )
        self.sends, self.receives = sends, receives

    def start(self):
        pl.when(self.sends)(self.copy.start)

    def sent(self):
        pl.when(self.sends)(self.copy.wait_send)

    def arrived(self):
        pl.when(self.receives)(self.copy.wait_recv)


class Halo:
    def __init__(self, own, regions, links, has, where):
        planes, width = own.shape[0], own.shape[-1]
        tall = width // CHUNKS
        beyond = slice(width, 2 * width)
        forwards = has["up"] & has["right"], has["down"] & has["right"]
        self.has = has
        self.across, self.down, self.corner = {}, {}, {}
        for plane in range(planes):
            for piece in range(CHUNKS):
                rows = slice(piece * tall, (piece + 1) * tall)
                under = slice(width + piece * tall, width + (piece + 1) * tall)
                mine = own.at[plane, rows]
                held = regions[plane // 2]
                right = held.at[plane % 2, rows, beyond]
                below = held.at[plane % 2, under, slice(0, width)]
                diagonal = held.at[plane % 2, under, beyond]
                key = plane, piece
                self.across[key] = links.link(
                    mine, right, where["left"], has["left"], has["right"]
                )
                self.down[key] = links.link(mine, below, where["up"], has["up"], has["down"])
                self.corner[key] = links.link(right, diagonal, where["up"], *forwards)

    def blank(self, region):
        has = self.has
        planes, width = region.shape[0], region.shape[-1] // 2
        upper, lower = slice(0, width), slice(width, 2 * width)
        zeros = jnp.zeros((planes, width, width), F32)

        @pl.when(jnp.logical_not(has["right"]))
        def _():
            region[:, upper, lower] = zeros

        @pl.when(jnp.logical_not(has["down"]))
        def _():
            region[:, lower, upper] = zeros

        @pl.when(jnp.logical_not(has["down"] & has["right"]))
        def _():
            region[:, lower, lower] = zeros

    def forward(self, plane, piece):
        self.across[plane, piece].arrived()
        self.corner[plane, piece].start()

    def finish(self, planes):
        for plane in planes:
            for piece in range(CHUNKS):
                self.down[plane, piece].arrived()
                self.corner[plane, piece].arrived()


class Sums:
    def __init__(self, totals, passing, got, links, has, where):
        self.totals, self.passing, self.got, self.has = totals, passing, got, has
        planes, width = passing.shape[0], passing.shape[-1]
        tall = width // CHUNKS
        self.corner, self.down, self.across = {}, {}, {}
        for plane in range(planes):
            for piece in range(CHUNKS):
                rows = slice(piece * tall, (piece + 1) * tall)
                under = slice(width + piece * tall, width + (piece + 1) * tall)
                self.corner[plane, piece] = links.link(
                    totals.at[plane, under, slice(width, 2 * width)],
                    got.at[0, plane, rows],
                    where["down"],
                    has["down"],
                    has["up"],
                )
                self.across[plane, piece] = links.link(
                    passing.at[plane, rows],
                    got.at[2, plane, rows],
                    where["right"],
                    has["right"],
                    has["left"],
                )
            self.down[plane] = links.link(
                totals.at[plane, slice(width, 2 * width), slice(0, width)],
                got.at[1, plane],
                where["down"],
                has["down"],
                has["up"],
            )

    def start(self, planes):
        for plane in planes:
            for piece in range(CHUNKS):
                self.corner[plane, piece].start()
        for plane in planes:
            self.down[plane].start()

    def turn(self, plane, piece):
        width = self.passing.shape[-1]
        tall = width // CHUNKS
        rows = slice(piece * tall, (piece + 1) * tall)
        self.corner[plane, piece].arrived()
        came = jnp.where(self.has["up"], self.got[0, plane, rows], 0.0)
        self.passing[plane, rows] = self.totals[plane, rows, width:] + came
        self.across[plane, piece].start()

    def finish(self, planes):
        for plane in planes:
            self.down[plane].arrived()
            for piece in range(CHUNKS):
                self.across[plane, piece].arrived()

    def total(self, plane):
        width = self.passing.shape[-1]
        above = jnp.where(self.has["up"], self.got[1, plane], 0.0)
        beside = jnp.where(self.has["left"], self.got[2, plane], 0.0)
        return self.totals[plane, :width, :width] + above + beside


def turn_of(phase):
    half = phase * 0.5
    square = half * half
    for at in range(7, -1, -1):
        sign = -1.0 if at % 2 else 1.0
        if at == 7:
            cosine, sine = sign * (1.0 / math.factorial(14)), sign * (1.0 / math.factorial(15))
        else:
            cosine = cosine * square + sign / math.factorial(2 * at)
            sine = sine * square + sign / math.factorial(2 * at + 1)
    sine = sine * half
    return 1.0 - 2.0 * sine * sine, 2.0 * sine * cosine


def even_odd(value):
    width = value.shape[0]
    high, low = split(value)
    rest = (value - high.astype(F32) - low.astype(F32)).astype(BF16)
    new = lax.broadcasted_iota(jnp.int32, (width, width), 0)
    old = lax.broadcasted_iota(jnp.int32, (width, width), 1)
    wanted = jnp.where(new < width // 2, 2 * new, 2 * new - width + 1)
    pick = jnp.where(old == wanted, 1.0, 0.0).astype(BF16)
    rows = jnp.dot(pick, jnp.concatenate([high, low, rest], axis=1), preferred_element_type=F32)
    old = lax.broadcasted_iota(jnp.int32, (width, width), 0)
    new = lax.broadcasted_iota(jnp.int32, (width, width), 1)
    wanted = jnp.where(new < width // 2, 2 * new, 2 * new - width + 1)
    pick = jnp.where(old == wanted, 1.0, 0.0).astype(BF16)
    return jnp.dot(
        rows.astype(BF16), jnp.concatenate([pick, pick, pick], axis=0), preferred_element_type=F32
    )


def window(region, plane, top, left):
    width = region.shape[-1] // 2
    base = (top >> 3) * 8
    rows = region[plane, pl.ds(base, width + 8), :]
    rows = pltpu.roll(rows, (2 * width - left) & (2 * width - 1), 1)[:, :width]
    return pltpu.roll(rows, lax.rem(width + 8 - (top & 7), width + 8), 0)[:width]


def deposit(padded, totals, planes, first, pieces, coords, live, shared=False):
    width = totals.shape[-1] // 2
    tall = 64
    slots = coords.shape[1]

    @pl.loop(*pieces)
    def _(piece):
        for plane in range(planes):
            total = jnp.zeros((tall, 2 * width), F32)
            for slot in range(slots):
                top, left = coords[0, slot], coords[1, slot]
                alive = jnp.minimum(jnp.maximum(live[0] - slot, 0), 1)
                start = (width - top + piece * tall) * alive
                base = (start >> 3) * 8
                rows = padded[0 if shared else slot, plane, pl.ds(base, tall + 8), :]
                rows = pltpu.roll(rows, lax.rem(tall + 8 - (start & 7), tall + 8), 0)[:tall]
                wide = jnp.concatenate([rows, jnp.zeros_like(rows)], axis=1)
                total += pltpu.roll(wide, left, 1)
            at = pl.multiple_of(piece * tall, tall)
            totals[first + plane, pl.ds(at, tall), :] = total


def stage(group, count, source, between, after, tables, hooks):
    forth, back = tables

    def run(step, place):
        for (at, spot), hook in hooks.items():
            if spot == place:
                pl.when(step == at)(hook)

    @pl.loop(0, count // group)
    def _(step):
        slots = [step * group + at for at in range(group)]
        inputs = [source(slot) for slot in slots]
        run(step, 0)
        spectra = to_spectrum(inputs, *forth)
        run(step, 1)
        moved = [between(slot, *pair) for slot, pair in zip(slots, spectra)]
        outs = from_spectrum(moved, *back)
        run(step, 2)
        for slot, pair in zip(slots, outs):
            after(slot, *pair)
        run(step, 3)


def kernel(group, coords, live, own, probe_in, phase_in, amplitude_in, left_in, right_in, *refs):
    norm_one, norm_two, grad_two, grad_one, *refs = refs
    one, two, probe, phase, amplitude, left_t, right_t, wave, patch, inner, *refs = refs
    padded, totals, passing, got, local, *sems = refs
    width = own.shape[-1]
    middle = slice(width, 2 * width)
    count = coords.shape[1]
    has, where = neighbours()
    greet(has, where)
    links = Links(sems)
    halo = Halo(own, (one, two), links, has, where)
    sums = Sums(totals, passing, got, links, has, where)
    pieces = range(CHUNKS)
    for plane in range(4):
        for piece in pieces:
            halo.across[plane, piece].start()
        if plane < 2:
            for piece in pieces:
                halo.down[plane, piece].start()
    fetches = [
        pltpu.make_async_copy(source, target, local.at[at])
        for at, (source, target) in enumerate(
            [
                (probe_in, probe),
                (phase_in, phase.at[0]),
                (amplitude_in, amplitude),
                (left_in, left_t),
                (right_in, right_t),
                (own.at[0:2], one.at[:, slice(0, width), slice(0, width)]),
                (own.at[2:4], two.at[:, slice(0, width), slice(0, width)]),
            ]
        )
    ]
    for fetch in fetches:
        fetch.start()
    margin = jnp.zeros((width, width), F32)

    @pl.loop(0, count)
    def _(slot):
        for plane in range(2):
            padded[slot, plane, slice(0, width)] = margin
            padded[slot, plane, slice(2 * width, 3 * width)] = margin
            padded[slot, plane, slice(3 * width, 3 * width + 8)] = margin[:8]

    fetches[0].wait()
    padded[0, 0, middle] = probe[0] * probe[0] + probe[1] * probe[1]
    upper, lower = (0, 2 * width // 128), (2 * width // 128, 2 * width // 64)
    deposit(padded, totals, 1, 0, lower, coords, live, shared=True)
    sums.start([0])
    deposit(padded, totals, 1, 0, upper, coords, live, shared=True)
    halo.blank(one)
    halo.blank(two)
    halo.forward(0, 0)
    fetches[1].wait()
    cosine, sine = turn_of(phase[0])
    phase[0], phase[1] = even_odd(cosine), even_odd(sine)
    halo.forward(0, 1)
    halo.down[2, 0].start()
    fetches[2].wait()

    @pl.loop(0, count)
    def _(slot):
        amplitude[slot] = even_odd(amplitude[slot])

    for piece in pieces:
        sums.turn(0, piece)
    halo.forward(1, 0)
    halo.forward(1, 1)
    halo.down[2, 1].start()
    for piece in pieces:
        halo.down[3, piece].start()
    for fetch in fetches[3:]:
        fetch.wait()
    halo.finish([0, 1])
    forth = [left_t.at[0], left_t.at[1]], [right_t.at[0], right_t.at[1]]
    back = [left_t.at[2], left_t.at[3]], [right_t.at[2], right_t.at[3]]
    tables = forth, back

    def first_source(slot):
        top, left = coords[0, slot], coords[1, slot]
        real, imag = window(one, 0, top, left), window(one, 1, top, left)
        return probe[0] * real - probe[1] * imag, probe[0] * imag + probe[1] * real

    def first_between(slot, real, imag):
        return real * phase[0] - imag * phase[1], real * phase[1] + imag * phase[0]

    def first_after(slot, real, imag):
        wave[slot, 0], wave[slot, 1] = real, imag
        padded[slot, 0, middle] = real * real + imag * imag

    last = count // group - 1
    hooks = {(0, 1): lambda: halo.forward(2, 0), (last, 1): lambda: halo.forward(2, 1)}
    stage(group, count, first_source, first_between, first_after, tables, hooks)
    deposit(padded, totals, 1, 1, lower, coords, live)
    sums.start([1])
    deposit(padded, totals, 1, 1, upper, coords, live)
    halo.forward(3, 0)
    halo.forward(3, 1)
    for piece in pieces:
        sums.turn(1, piece)
    halo.finish([2, 3])

    def second_source(slot):
        top, left = coords[0, slot], coords[1, slot]
        second_r, second_i = window(two, 0, top, left), window(two, 1, top, left)
        patch[slot, 0], patch[slot, 1] = second_r, second_i
        wave_r, wave_i = wave[slot, 0], wave[slot, 1]
        return wave_r * second_r - wave_i * second_i, wave_r * second_i + wave_i * second_r

    def second_between(slot, real, imag):
        size = jnp.minimum(lax.rsqrt(real * real + imag * imag), 2.0)
        ratio = amplitude[slot] * size - 1.0
        return real * ratio, imag * ratio

    def second_after(slot, real, imag):
        second_r, second_i = patch[slot, 0], patch[slot, 1]
        inner[slot, 0] = second_r * real + second_i * imag
        inner[slot, 1] = second_r * imag - second_i * real
        wave_r, wave_i = wave[slot, 0], wave[slot, 1]
        padded[slot, 0, middle] = wave_r * real + wave_i * imag
        padded[slot, 1, middle] = wave_r * imag - wave_i * real

    stage(group, count, second_source, second_between, second_after, tables, {})
    deposit(padded, totals, 2, 2, lower, coords, live)
    sums.start([2, 3])
    deposit(padded, totals, 2, 2, upper, coords, live)

    def third_between(slot, real, imag):
        return real * phase[0] + imag * phase[1], imag * phase[0] - real * phase[1]

    def third_after(slot, real, imag):
        padded[slot, 0, middle] = probe[0] * real + probe[1] * imag
        padded[slot, 1, middle] = probe[0] * imag - probe[1] * real

    def turn_both(plane):
        def turns():
            for piece in pieces:
                sums.turn(plane, piece)

        return turns

    hooks = {(0, 1): turn_both(2), (last, 1 if last else 3): turn_both(3)}
    stage(
        group,
        count,
        lambda slot: (inner[slot, 0], inner[slot, 1]),
        third_between,
        third_after,
        tables,
        hooks,
    )
    deposit(padded, totals, 2, 4, lower, coords, live)
    sums.start([4, 5])
    deposit(padded, totals, 2, 4, upper, coords, live)
    for plane in (4, 5):
        for piece in pieces:
            sums.turn(plane, piece)
    sums.finish([0, 1, 2, 3])
    norm_one[...], norm_two[...] = sums.total(0), sums.total(1)
    grad_two[0], grad_two[1] = sums.total(2), sums.total(3)
    sums.finish([4, 5])
    grad_one[0], grad_one[1] = sums.total(4), sums.total(5)
    links.sent()


def on_device(object_planes, probe, phase, coords, live, amplitude):
    width = probe.shape[-1]
    slots = coords.shape[2]
    group = 2 if slots % 2 == 0 else 1
    left_t, right_t = dft_tables(width)
    smem = pl.BlockSpec(memory_space=pltpu.SMEM)
    hbm = pl.BlockSpec(memory_space=pltpu.HBM)
    vmem = pl.BlockSpec(memory_space=pltpu.VMEM)

    def planes(*lead):
        return jax.ShapeDtypeStruct((*lead, width, width), F32)

    def scratch(*shape):
        return pltpu.VMEM((*shape, width, width), F32)

    links = 4 * 3 * CHUNKS + 6 * (2 * CHUNKS + 1)
    outs = [planes(), planes(), planes(2), planes(2)]

    def bound(*refs):
        kernel(group, *refs)

    norm_one, norm_two, grad_two, grad_one = pl.pallas_call(
        bound,
        out_shape=outs,
        in_specs=[smem] * 2 + [hbm] * 6,
        out_specs=[vmem] * 4,
        scratch_shapes=[
            pltpu.VMEM((2, 2 * width, 2 * width), F32),
            pltpu.VMEM((2, 2 * width, 2 * width), F32),
            scratch(2),
            scratch(2),
            scratch(slots),
            pltpu.VMEM(left_t.shape, BF16),
            pltpu.VMEM(right_t.shape, BF16),
            scratch(slots, 2),
            scratch(slots, 2),
            scratch(slots, 2),
            pltpu.VMEM((slots, 2, 3 * width + 8, width), F32),
            pltpu.VMEM((6, 2 * width, 2 * width), F32),
            scratch(6),
            scratch(3, 6),
            pltpu.SemaphoreType.DMA((7,)),
            pltpu.SemaphoreType.DMA((links,)),
            pltpu.SemaphoreType.DMA((links,)),
        ],
        compiler_params=pltpu.CompilerParams(
            vmem_limit_bytes=60 << 20, collective_id=0, has_side_effects=True
        ),
        cost_estimate=pl.CostEstimate(
            flops=48 * slots * width**3, bytes_accessed=8 << 20, transcendentals=0
        ),
        name="iteration",
    )(coords[0, 0].T, live[0], object_planes, probe, phase, amplitude[0, 0], left_t, right_t)
    new_first = object_planes[0:2] + grad_one / (norm_one + 1.0)
    new_second = object_planes[2:4] + grad_two / (norm_two + 1.0)
    return jnp.concatenate([new_first, new_second])


def solution(mesh):
    return jax.shard_map(
        on_device,
        mesh=mesh,
        in_specs=(
            P(None, ("groups", "ty"), "tx"),
            P(),
            P(),
            P(("groups", "ty"), "tx", None, None),
            P(("groups", "ty"), "tx"),
            P(("groups", "ty"), "tx", None, None, None),
        ),
        out_specs=P(None, ("groups", "ty"), "tx"),
        check_vma=False,
    )
```

```python
import math

import jax
import jax.numpy as jnp
import numpy as np
from jax import lax
from jax.experimental import pallas as pl
from jax.experimental.pallas import tpu as pltpu
from jax.sharding import PartitionSpec as P

F32 = jnp.float32
BF16 = jnp.bfloat16
CHUNKS = 2


def dft_tables(width):
    half = width // 2
    scale = 1.0 / math.sqrt(width)

    def stacked(table, axis):
        table = table.astype(np.float32)
        high = table.astype(BF16)
        low = (table - high.astype(np.float32)).astype(BF16)
        return np.concatenate([high, high, low], axis=axis)

    lefts, rights = [], []
    for parity in range(2):
        index = (2 * np.arange(half) + parity)[:, None] * np.arange(half)[None, :] % width
        angles = index * (2.0 * math.pi / width)
        real, imag = np.cos(angles) * scale, -np.sin(angles) * scale
        whole = np.block([[real, -imag], [imag, real]])
        lefts.append((stacked(whole, 1), stacked(whole.T, 1)))
        rights.append((stacked(whole.T, 0), stacked(whole, 0)))
    left = np.stack([lefts[parity][way] for way in range(2) for parity in range(2)])
    right = np.stack([rights[parity][way] for way in range(2) for parity in range(2)])
    return jnp.asarray(left), jnp.asarray(right)


def split(value):
    high = value.astype(BF16)
    low = (value - high.astype(F32)).astype(BF16)
    return high, low


def tripled(value, axis):
    high, low = split(value)
    return jnp.concatenate([high, low, high], axis=axis)


def to_spectrum(values, left, right):
    width = values[0][0].shape[0]
    half = width // 2
    sides = []
    for parity in range(2):
        columns = []
        for pair in values:
            parts = [v[:half] - v[half:] if parity else v[:half] + v[half:] for v in pair]
            columns.append(tripled(jnp.concatenate(parts, axis=0), 0))
        data = jnp.concatenate(columns, axis=1)
        sides.append(jnp.dot(left[parity][...], data, preferred_element_type=F32))
    outs = []
    for parity in range(2):
        rows = []
        for at in range(len(values)):
            cut = slice(at * width, (at + 1) * width)
            parts = []
            for part in (slice(0, half), slice(half, width)):
                v = jnp.concatenate([sides[0][part, cut], sides[1][part, cut]], axis=0)
                parts.append(v[:, :half] - v[:, half:] if parity else v[:, :half] + v[:, half:])
            rows.append(tripled(jnp.concatenate(parts, axis=1), 1))
        data = jnp.concatenate(rows, axis=0)
        outs.append(jnp.dot(data, right[parity][...], preferred_element_type=F32))
    result = []
    for at in range(len(values)):
        rows = slice(at * width, (at + 1) * width)
        real = jnp.concatenate([outs[0][rows, :half], outs[1][rows, :half]], axis=1)
        imag = jnp.concatenate([outs[0][rows, half:], outs[1][rows, half:]], axis=1)
        result.append((real, imag))
    return result


def from_spectrum(values, left, right):
    width = values[0][0].shape[0]
    half = width // 2
    halves = (slice(0, half), slice(half, width))
    sides = []
    for parity in range(2):
        columns = []
        for pair in values:
            parts = [v[halves[parity]] for v in pair]
            columns.append(tripled(jnp.concatenate(parts, axis=0), 0))
        data = jnp.concatenate(columns, axis=1)
        sides.append(jnp.dot(left[parity][...], data, preferred_element_type=F32))
    tops = sides[0] + sides[1]
    lows = sides[0] - sides[1]
    outs = []
    for parity in range(2):
        rows = []
        for at in range(len(values)):
            cut = slice(at * width + parity * half, at * width + (parity + 1) * half)
            parts = [
                jnp.concatenate([tops[part, cut], lows[part, cut]], axis=0) for part in halves
            ]
            rows.append(tripled(jnp.concatenate(parts, axis=1), 1))
        data = jnp.concatenate(rows, axis=0)
        outs.append(jnp.dot(data, right[parity][...], preferred_element_type=F32))
    total, gap = outs[0] + outs[1], outs[0] - outs[1]
    result = []
    for at in range(len(values)):
        rows = slice(at * width, (at + 1) * width)
        real = jnp.concatenate([total[rows, :half], gap[rows, :half]], axis=1)
        imag = jnp.concatenate([total[rows, half:], gap[rows, half:]], axis=1)
        result.append((real, imag))
    return result


def neighbours():
    row, column = lax.axis_index("ty"), lax.axis_index("tx")
    has = {
        "up": row > 0,
        "down": row < lax.axis_size("ty") - 1,
        "left": column > 0,
        "right": column < lax.axis_size("tx") - 1,
    }
    where = {
        "up": {"ty": row - 1},
        "down": {"ty": row + 1},
        "left": {"tx": column - 1},
        "right": {"tx": column + 1},
    }
    return has, where


def greet(has, where):
    barrier = pltpu.get_barrier_semaphore()
    for side, there in has.items():

        @pl.when(there)
        def _():
            pl.semaphore_signal(
                barrier, inc=1, device_id=where[side], device_id_type=pl.DeviceIdType.MESH
            )

    peers = sum(there.astype(jnp.int32) for there in has.values())
    pl.semaphore_wait(barrier, peers)


class Links:
    def __init__(self, sems):
        self.sems, self.every = sems, []

    def link(self, source, target, device, sends, receives):
        at = len(self.every)
        made = Link(source, target, self.sems, at, device, sends, receives)
        self.every.append(made)
        return made

    def sent(self):
        for made in self.every:
            made.sent()


class Link:
    def __init__(self, source, target, sems, at, device, sends, receives):
        self.copy = pltpu.make_async_remote_copy(
            src_ref=source,
            dst_ref=target,
            send_sem=sems[0].at[at],
            recv_sem=sems[1].at[at],
            device_id=device,
            device_id_type=pl.DeviceIdType.MESH,
        )
        self.sends, self.receives = sends, receives

    def start(self):
        pl.when(self.sends)(self.copy.start)

    def sent(self):
        pl.when(self.sends)(self.copy.wait_send)

    def arrived(self):
        pl.when(self.receives)(self.copy.wait_recv)


class Halo:
    def __init__(self, own, regions, links, has, where):
        planes, width = own.shape[0], own.shape[-1]
        tall = width // CHUNKS
        forwards = has["up"] & has["right"], has["down"] & has["right"]
        self.has = has
        self.across, self.down, self.corner = {}, {}, {}
        for plane in range(planes):
            for piece in range(CHUNKS):
                rows = slice(piece * tall, (piece + 1) * tall)
                mine = own.at[plane, rows]
                right, below, diagonal = [
                    regions[plane // 2].at[plane % 2, quarter, rows] for quarter in (1, 2, 3)
                ]
                key = plane, piece
                self.across[key] = links.link(
                    mine, right, where["left"], has["left"], has["right"]
                )
                self.down[key] = links.link(mine, below, where["up"], has["up"], has["down"])
                self.corner[key] = links.link(right, diagonal, where["up"], *forwards)

    def blank(self, region):
        has = self.has
        zeros = jnp.zeros(region.shape[2:], F32)
        there = has["right"], has["down"], has["down"] & has["right"]
        for plane in range(2):
            for quarter in (1, 2, 3):

                @pl.when(jnp.logical_not(there[quarter - 1]))
                def _():
                    region[plane, quarter] = zeros

    def forward(self, plane, piece):
        self.across[plane, piece].arrived()
        self.corner[plane, piece].start()

    def finish(self, planes):
        for plane in planes:
            for piece in range(CHUNKS):
                self.down[plane, piece].arrived()
                self.corner[plane, piece].arrived()


class Sums:
    def __init__(self, totals, passing, got, links, has, where):
        self.totals, self.passing, self.got, self.has = totals, passing, got, has
        planes, width = passing.shape[0], passing.shape[-1]
        tall = width // CHUNKS
        self.corner, self.down, self.across = {}, {}, {}
        for plane in range(planes):
            for piece in range(CHUNKS):
                rows = slice(piece * tall, (piece + 1) * tall)
                self.corner[plane, piece] = links.link(
                    totals.at[plane, 3, rows],
                    got.at[0, plane, rows],
                    where["down"],
                    has["down"],
                    has["up"],
                )
                self.across[plane, piece] = links.link(
                    passing.at[plane, rows],
                    got.at[2, plane, rows],
                    where["right"],
                    has["right"],
                    has["left"],
                )
            self.down[plane] = links.link(
                totals.at[plane, 2], got.at[1, plane], where["down"], has["down"], has["up"]
            )

    def start(self, planes):
        for plane in planes:
            for piece in range(CHUNKS):
                self.corner[plane, piece].start()
        for plane in planes:
            self.down[plane].start()

    def turn(self, plane, piece):
        tall = self.passing.shape[-1] // CHUNKS
        rows = slice(piece * tall, (piece + 1) * tall)
        self.corner[plane, piece].arrived()
        came = jnp.where(self.has["up"], self.got[0, plane, rows], 0.0)
        self.passing[plane, rows] = self.totals[plane, 1, rows] + came
        self.across[plane, piece].start()

    def finish(self, planes):
        for plane in planes:
            self.down[plane].arrived()
            for piece in range(CHUNKS):
                self.across[plane, piece].arrived()

    def total(self, plane):
        above = jnp.where(self.has["up"], self.got[1, plane], 0.0)
        beside = jnp.where(self.has["left"], self.got[2, plane], 0.0)
        return self.totals[plane, 0] + above + beside


def turn_of(phase):
    half = phase * 0.5
    square = half * half
    for at in range(7, -1, -1):
        sign = -1.0 if at % 2 else 1.0
        if at == 7:
            cosine, sine = sign * (1.0 / math.factorial(14)), sign * (1.0 / math.factorial(15))
        else:
            cosine = cosine * square + sign / math.factorial(2 * at)
            sine = sine * square + sign / math.factorial(2 * at + 1)
    sine = sine * half
    return 1.0 - 2.0 * sine * sine, 2.0 * sine * cosine


def even_odd(value):
    width = value.shape[0]
    high, low = split(value)
    rest = (value - high.astype(F32) - low.astype(F32)).astype(BF16)
    new = lax.broadcasted_iota(jnp.int32, (width, width), 0)
    old = lax.broadcasted_iota(jnp.int32, (width, width), 1)
    wanted = jnp.where(new < width // 2, 2 * new, 2 * new - width + 1)
    pick = jnp.where(old == wanted, 1.0, 0.0).astype(BF16)
    rows = jnp.dot(pick, jnp.concatenate([high, low, rest], axis=1), preferred_element_type=F32)
    old = lax.broadcasted_iota(jnp.int32, (width, width), 0)
    new = lax.broadcasted_iota(jnp.int32, (width, width), 1)
    wanted = jnp.where(new < width // 2, 2 * new, 2 * new - width + 1)
    pick = jnp.where(old == wanted, 1.0, 0.0).astype(BF16)
    return jnp.dot(
        rows.astype(BF16), jnp.concatenate([pick, pick, pick], axis=0), preferred_element_type=F32
    )


def place(shape, coords, slot, row=0):
    rows = lax.broadcasted_iota(jnp.int32, shape, 0) + row
    columns = lax.broadcasted_iota(jnp.int32, shape, 1)
    return rows >= coords[0, slot], columns >= coords[1, slot]


def window(region, coords, slot):
    rows, columns = place(region.shape[2:], coords, slot)
    return [
        jnp.where(
            columns,
            jnp.where(rows, region[plane, 0], region[plane, 2]),
            jnp.where(rows, region[plane, 1], region[plane, 3]),
        )
        for plane in range(2)
    ]


def deposit(source, totals, first, coords):
    width = totals.shape[-1]
    tall = 32

    @pl.loop(0, width // tall)
    def _(piece):
        at = pl.ds(pl.multiple_of(piece * tall, tall), tall)
        sums = None
        for slot in range(coords.shape[1]):
            rows, columns = place((tall, width), coords, slot, piece * tall)
            parts = []
            for value in source(slot, at):
                left, right = jnp.where(columns, value, 0.0), jnp.where(columns, 0.0, value)
                for side, mask in ((left, rows), (right, rows)):
                    parts.append(jnp.where(mask, side, 0.0))
                for side, mask in ((left, rows), (right, rows)):
                    parts.append(jnp.where(mask, 0.0, side))
            sums = parts if sums is None else [a + b for a, b in zip(sums, parts)]
        for index, total in enumerate(sums):
            totals[first + index // 4, index % 4, at] = total


def stage(group, count, source, between, after, tables, hooks):
    forth, back = tables

    def run(step, place):
        for (at, spot), hook in hooks.items():
            if spot == place:
                pl.when(step == at)(hook)

    @pl.loop(0, count // group)
    def _(step):
        slots = [step * group + at for at in range(group)]
        inputs = [source(slot) for slot in slots]
        run(step, 0)
        spectra = to_spectrum(inputs, *forth)
        run(step, 1)
        moved = [between(slot, *pair) for slot, pair in zip(slots, spectra)]
        outs = from_spectrum(moved, *back)
        run(step, 2)
        for slot, pair in zip(slots, outs):
            after(slot, *pair)
        run(step, 3)


def kernel(group, coords, live, own, probe_in, phase_in, amplitude_in, left_in, right_in, *refs):
    updated, one, two, twice, phase, amplitude, left_t, right_t, probe, wave, back, *refs = refs
    inverse, totals, passing, got, local, *sems = refs
    width = own.shape[-1]
    count = coords.shape[1]
    has, where = neighbours()
    greet(has, where)
    links = Links(sems)
    halo = Halo(own, (one, two), links, has, where)
    sums = Sums(totals, passing, got, links, has, where)
    pieces = range(CHUNKS)
    for plane in range(4):
        for piece in pieces:
            halo.across[plane, piece].start()
        if plane < 2:
            for piece in pieces:
                halo.down[plane, piece].start()
    fetches = [
        pltpu.make_async_copy(source, target, local.at[at])
        for at, (source, target) in enumerate(
            [
                (probe_in, twice.at[:, slice(0, width)]),
                (probe_in, twice.at[:, slice(width, 2 * width)]),
                (phase_in, phase.at[0]),
                (amplitude_in, amplitude),
                (left_in, left_t),
                (right_in, right_t),
                (own.at[0:2], one.at[:, 0]),
                (own.at[2:4], two.at[:, 0]),
            ]
        )
    ]
    for fetch in fetches:
        fetch.start()
    for fetch in fetches[:2]:
        fetch.wait()

    @pl.loop(0, count)
    def _(slot):
        top, left = coords[0, slot], coords[1, slot]
        alive = jnp.minimum(jnp.maximum(live[0] - slot, 0), 1).astype(F32)
        start = width - top
        for plane in range(2):
            rows = twice[plane, pl.ds((start >> 3) * 8, width + 8), :]
            rows = pltpu.roll(rows, lax.rem(width + 8 - (start & 7), width + 8), 0)[:width]
            probe[slot, plane] = pltpu.roll(rows, left, 1) * alive

    def power(of):
        def source(slot, rows):
            real, imag = of[slot, 0, rows], of[slot, 1, rows]
            return [real * real + imag * imag]

        return source

    def crossed(of, by):
        def source(slot, rows):
            real, imag = by[slot, 0, rows], by[slot, 1, rows]
            first, second = of[slot, 0, rows], of[slot, 1, rows]
            return [first * real + second * imag, first * imag - second * real]

        return source

    deposit(power(probe), totals, 0, coords)
    sums.start([0])
    halo.blank(one)
    halo.blank(two)
    halo.forward(0, 0)
    fetches[2].wait()
    cosine, sine = turn_of(phase[0])
    phase[0], phase[1] = even_odd(cosine), even_odd(sine)
    halo.forward(0, 1)
    halo.down[2, 0].start()
    fetches[3].wait()

    @pl.loop(0, count)
    def _(slot):
        amplitude[slot] = even_odd(amplitude[slot])

    for piece in pieces:
        sums.turn(0, piece)
    halo.forward(1, 0)
    halo.forward(1, 1)
    halo.down[2, 1].start()
    for piece in pieces:
        halo.down[3, piece].start()
    for fetch in fetches[4:]:
        fetch.wait()
    halo.finish([0, 1])
    forth = [left_t.at[0], left_t.at[1]], [right_t.at[0], right_t.at[1]]
    tables = forth, ([left_t.at[2], left_t.at[3]], [right_t.at[2], right_t.at[3]])

    def first_source(slot):
        real, imag = window(one, coords, slot)
        probe_r, probe_i = probe[slot, 0], probe[slot, 1]
        return probe_r * real - probe_i * imag, probe_r * imag + probe_i * real

    def first_between(slot, real, imag):
        return real * phase[0] - imag * phase[1], real * phase[1] + imag * phase[0]

    def keep(target):
        def after(slot, real, imag):
            target[slot, 0], target[slot, 1] = real, imag

        return after

    last = count // group - 1
    hooks = {(0, 1): lambda: halo.forward(2, 0), (last, 1): lambda: halo.forward(2, 1)}
    stage(group, count, first_source, first_between, keep(wave), tables, hooks)
    deposit(power(wave), totals, 1, coords)
    sums.start([1])
    halo.forward(3, 0)
    halo.forward(3, 1)
    for piece in pieces:
        sums.turn(1, piece)
    halo.finish([2, 3])

    def second_source(slot):
        second_r, second_i = window(two, coords, slot)
        wave_r, wave_i = wave[slot, 0], wave[slot, 1]
        return wave_r * second_r - wave_i * second_i, wave_r * second_i + wave_i * second_r

    def second_between(slot, real, imag):
        size = jnp.minimum(lax.rsqrt(real * real + imag * imag), 2.0)
        ratio = amplitude[slot] * size - 1.0
        return real * ratio, imag * ratio

    stage(group, count, second_source, second_between, keep(back), tables, {})
    deposit(crossed(wave, back), totals, 2, coords)
    sums.start([2, 3])

    def third_source(slot):
        second_r, second_i = window(two, coords, slot)
        real, imag = back[slot, 0], back[slot, 1]
        return second_r * real + second_i * imag, second_r * imag - second_i * real

    def third_between(slot, real, imag):
        return real * phase[0] + imag * phase[1], imag * phase[0] - real * phase[1]

    def turn_both(plane):
        def turns():
            for piece in pieces:
                sums.turn(plane, piece)

        return turns

    hooks = {(0, 1): turn_both(2), (last, 1 if last else 3): turn_both(3)}
    stage(group, count, third_source, third_between, keep(back), tables, hooks)
    deposit(crossed(probe, back), totals, 4, coords)
    sums.start([4, 5])
    for plane in (4, 5):
        for piece in pieces:
            sums.turn(plane, piece)
    sums.finish([0, 1, 2, 3])
    inverse[...] = 1.0 / (sums.total(0) + 1.0)
    for plane in range(2):
        updated[2 + plane] = two[plane, 0] + sums.total(2 + plane) / (sums.total(1) + 1.0)
    sums.finish([4, 5])
    for plane in range(2):
        updated[plane] = one[plane, 0] + sums.total(4 + plane) * inverse[...]
    links.sent()


def on_device(object_planes, probe, phase, coords, live, amplitude):
    width = probe.shape[-1]
    slots = coords.shape[2]
    group = 2 if slots % 2 == 0 else 1
    left_t, right_t = dft_tables(width)
    smem = pl.BlockSpec(memory_space=pltpu.SMEM)
    hbm = pl.BlockSpec(memory_space=pltpu.HBM)
    vmem = pl.BlockSpec(memory_space=pltpu.VMEM)

    def scratch(*shape):
        return pltpu.VMEM((*shape, width, width), F32)

    links = 4 * 3 * CHUNKS + 6 * (2 * CHUNKS + 1)

    def bound(*refs):
        kernel(group, *refs)

    return pl.pallas_call(
        bound,
        out_shape=jax.ShapeDtypeStruct(object_planes.shape, F32),
        in_specs=[smem] * 2 + [hbm] * 6,
        out_specs=vmem,
        scratch_shapes=[
            scratch(2, 4),
            scratch(2, 4),
            pltpu.VMEM((2, 2 * width + 8, width), F32),
            scratch(2),
            scratch(slots),
            pltpu.VMEM(left_t.shape, BF16),
            pltpu.VMEM(right_t.shape, BF16),
            scratch(slots, 2),
            scratch(slots, 2),
            scratch(slots, 2),
            scratch(),
            scratch(6, 4),
            scratch(6),
            scratch(3, 6),
            pltpu.SemaphoreType.DMA((8,)),
            pltpu.SemaphoreType.DMA((links,)),
            pltpu.SemaphoreType.DMA((links,)),
        ],
        compiler_params=pltpu.CompilerParams(
            vmem_limit_bytes=60 << 20, collective_id=0, has_side_effects=True
        ),
        cost_estimate=pl.CostEstimate(
            flops=48 * slots * width**3, bytes_accessed=8 << 20, transcendentals=0
        ),
        name="iteration",
    )(coords[0, 0].T, live[0], object_planes, probe, phase, amplitude[0, 0], left_t, right_t)


def solution(mesh):
    return jax.shard_map(
        on_device,
        mesh=mesh,
        in_specs=(
            P(None, ("groups", "ty"), "tx"),
            P(),
            P(),
            P(("groups", "ty"), "tx", None, None),
            P(("groups", "ty"), "tx"),
            P(("groups", "ty"), "tx", None, None, None),
        ),
        out_specs=P(None, ("groups", "ty"), "tx"),
        check_vma=False,
    )
```

```python
import math

import jax
import jax.numpy as jnp
import numpy as np
from jax import lax
from jax.experimental import pallas as pl
from jax.experimental.pallas import tpu as pltpu
from jax.sharding import PartitionSpec as P

F32 = jnp.float32
BF16 = jnp.bfloat16
CHUNKS = 2


def dft_tables(width):
    half = width // 2
    scale = 1.0 / math.sqrt(width)

    def stacked(table, axis):
        table = table.astype(np.float32)
        high = table.astype(BF16)
        low = (table - high.astype(np.float32)).astype(BF16)
        return np.concatenate([high, high, low], axis=axis)

    lefts, rights = [], []
    for parity in range(2):
        index = (2 * np.arange(half) + parity)[:, None] * np.arange(half)[None, :] % width
        angles = index * (2.0 * math.pi / width)
        real, imag = np.cos(angles) * scale, -np.sin(angles) * scale
        whole = np.block([[real, -imag], [imag, real]])
        lefts.append((stacked(whole, 1), stacked(whole.T, 1)))
        rights.append((stacked(whole.T, 0), stacked(whole, 0)))
    left = np.stack([lefts[parity][way] for way in range(2) for parity in range(2)])
    right = np.stack([rights[parity][way] for way in range(2) for parity in range(2)])
    return jnp.asarray(left), jnp.asarray(right)


def split(value):
    high = value.astype(BF16)
    low = (value - high.astype(F32)).astype(BF16)
    return high, low


def tripled(value, axis):
    high, low = split(value)
    return jnp.concatenate([high, low, high], axis=axis)


def to_spectrum(values, left, right):
    width = values[0][0].shape[0]
    half = width // 2
    sides = []
    for parity in range(2):
        columns = []
        for pair in values:
            parts = [v[:half] - v[half:] if parity else v[:half] + v[half:] for v in pair]
            columns.append(tripled(jnp.concatenate(parts, axis=0), 0))
        data = jnp.concatenate(columns, axis=1)
        sides.append(jnp.dot(left[parity][...], data, preferred_element_type=F32))
    outs = []
    for parity in range(2):
        rows = []
        for at in range(len(values)):
            cut = slice(at * width, (at + 1) * width)
            parts = []
            for part in (slice(0, half), slice(half, width)):
                v = jnp.concatenate([sides[0][part, cut], sides[1][part, cut]], axis=0)
                parts.append(v[:, :half] - v[:, half:] if parity else v[:, :half] + v[:, half:])
            rows.append(tripled(jnp.concatenate(parts, axis=1), 1))
        data = jnp.concatenate(rows, axis=0)
        outs.append(jnp.dot(data, right[parity][...], preferred_element_type=F32))
    result = []
    for at in range(len(values)):
        rows = slice(at * width, (at + 1) * width)
        real = jnp.concatenate([outs[0][rows, :half], outs[1][rows, :half]], axis=1)
        imag = jnp.concatenate([outs[0][rows, half:], outs[1][rows, half:]], axis=1)
        result.append((real, imag))
    return result


def from_spectrum(values, left, right):
    width = values[0][0].shape[0]
    half = width // 2
    halves = (slice(0, half), slice(half, width))
    sides = []
    for parity in range(2):
        columns = []
        for pair in values:
            parts = [v[halves[parity]] for v in pair]
            columns.append(tripled(jnp.concatenate(parts, axis=0), 0))
        data = jnp.concatenate(columns, axis=1)
        sides.append(jnp.dot(left[parity][...], data, preferred_element_type=F32))
    tops = sides[0] + sides[1]
    lows = sides[0] - sides[1]
    outs = []
    for parity in range(2):
        rows = []
        for at in range(len(values)):
            cut = slice(at * width + parity * half, at * width + (parity + 1) * half)
            parts = [
                jnp.concatenate([tops[part, cut], lows[part, cut]], axis=0) for part in halves
            ]
            rows.append(tripled(jnp.concatenate(parts, axis=1), 1))
        data = jnp.concatenate(rows, axis=0)
        outs.append(jnp.dot(data, right[parity][...], preferred_element_type=F32))
    total, gap = outs[0] + outs[1], outs[0] - outs[1]
    result = []
    for at in range(len(values)):
        rows = slice(at * width, (at + 1) * width)
        real = jnp.concatenate([total[rows, :half], gap[rows, :half]], axis=1)
        imag = jnp.concatenate([total[rows, half:], gap[rows, half:]], axis=1)
        result.append((real, imag))
    return result


def neighbours():
    row, column = lax.axis_index("ty"), lax.axis_index("tx")
    has = {
        "up": row > 0,
        "down": row < lax.axis_size("ty") - 1,
        "left": column > 0,
        "right": column < lax.axis_size("tx") - 1,
    }
    where = {
        "up": {"ty": row - 1},
        "down": {"ty": row + 1},
        "left": {"tx": column - 1},
        "right": {"tx": column + 1},
    }
    return has, where


def greet(has, where):
    barrier = pltpu.get_barrier_semaphore()
    for side, there in has.items():

        @pl.when(there)
        def _():
            pl.semaphore_signal(
                barrier, inc=1, device_id=where[side], device_id_type=pl.DeviceIdType.MESH
            )

    peers = sum(there.astype(jnp.int32) for there in has.values())
    pl.semaphore_wait(barrier, peers)


class Links:
    def __init__(self, sems):
        self.sems, self.every = sems, []

    def link(self, source, target, device, sends, receives):
        at = len(self.every)
        made = Link(source, target, self.sems, at, device, sends, receives)
        self.every.append(made)
        return made

    def sent(self, but):
        for made in self.every:
            if made not in but:
                made.sent()


class Link:
    def __init__(self, source, target, sems, at, device, sends, receives):
        self.copy = pltpu.make_async_remote_copy(
            src_ref=source,
            dst_ref=target,
            send_sem=sems[0].at[at],
            recv_sem=sems[1].at[at],
            device_id=device,
            device_id_type=pl.DeviceIdType.MESH,
        )
        self.sends, self.receives = sends, receives

    def start(self):
        pl.when(self.sends)(self.copy.start)

    def sent(self):
        pl.when(self.sends)(self.copy.wait_send)

    def arrived(self):
        pl.when(self.receives)(self.copy.wait_recv)


class Halo:
    def __init__(self, own, regions, links, has, where):
        planes, width = own.shape[0], own.shape[-1]
        tall = width // CHUNKS
        forwards = has["up"] & has["right"], has["down"] & has["right"]
        self.has = has
        self.across, self.down, self.corner = {}, {}, {}
        for plane in range(planes):
            for piece in range(CHUNKS):
                rows = slice(piece * tall, (piece + 1) * tall)
                mine = own.at[plane, rows]
                right, below, diagonal = [
                    regions[plane // 2].at[plane % 2, quarter, rows] for quarter in (1, 2, 3)
                ]
                key = plane, piece
                self.across[key] = links.link(
                    mine, right, where["left"], has["left"], has["right"]
                )
                self.down[key] = links.link(mine, below, where["up"], has["up"], has["down"])
                self.corner[key] = links.link(right, diagonal, where["up"], *forwards)

    def blank(self, region):
        has = self.has
        zeros = jnp.zeros(region.shape[2:], F32)
        there = has["right"], has["down"], has["down"] & has["right"]
        for plane in range(2):
            for quarter in (1, 2, 3):

                @pl.when(jnp.logical_not(there[quarter - 1]))
                def _():
                    region[plane, quarter] = zeros

    def forward(self, plane, piece):
        self.across[plane, piece].arrived()
        self.corner[plane, piece].start()

    def finish(self, planes):
        for plane in planes:
            for piece in range(CHUNKS):
                self.down[plane, piece].arrived()
                self.corner[plane, piece].arrived()


class Sums:
    def __init__(self, totals, passing, got, links, has, where):
        self.totals, self.passing, self.got, self.has = totals, passing, got, has
        planes, width = passing.shape[0], passing.shape[-1]
        tall = width // CHUNKS
        self.corner, self.down, self.across = {}, {}, {}
        for plane in range(planes):
            for piece in range(CHUNKS):
                rows = slice(piece * tall, (piece + 1) * tall)
                self.corner[plane, piece] = links.link(
                    totals.at[plane, 3, rows],
                    got.at[0, plane, rows],
                    where["down"],
                    has["down"],
                    has["up"],
                )
                self.across[plane, piece] = links.link(
                    passing.at[plane, rows],
                    got.at[2, plane, rows],
                    where["right"],
                    has["right"],
                    has["left"],
                )
            self.down[plane] = links.link(
                totals.at[plane, 2], got.at[1, plane], where["down"], has["down"], has["up"]
            )

    def start(self, planes):
        for plane in planes:
            for piece in range(CHUNKS):
                self.corner[plane, piece].start()
        for plane in planes:
            self.down[plane].start()

    def turn(self, plane, piece):
        tall = self.passing.shape[-1] // CHUNKS
        rows = slice(piece * tall, (piece + 1) * tall)
        self.corner[plane, piece].arrived()
        came = jnp.where(self.has["up"], self.got[0, plane, rows], 0.0)
        self.passing[plane, rows] = self.totals[plane, 1, rows] + came
        self.across[plane, piece].start()

    def finish(self, planes):
        for plane in planes:
            self.down[plane].arrived()
            for piece in range(CHUNKS):
                self.across[plane, piece].arrived()

    def total(self, plane):
        above = jnp.where(self.has["up"], self.got[1, plane], 0.0)
        beside = jnp.where(self.has["left"], self.got[2, plane], 0.0)
        return self.totals[plane, 0] + above + beside


def turn_of(phase):
    half = phase * 0.5
    square = half * half
    for at in range(7, -1, -1):
        sign = -1.0 if at % 2 else 1.0
        if at == 7:
            cosine, sine = sign * (1.0 / math.factorial(14)), sign * (1.0 / math.factorial(15))
        else:
            cosine = cosine * square + sign / math.factorial(2 * at)
            sine = sine * square + sign / math.factorial(2 * at + 1)
    sine = sine * half
    return 1.0 - 2.0 * sine * sine, 2.0 * sine * cosine


def even_odd(value):
    width = value.shape[0]
    high, low = split(value)
    rest = (value - high.astype(F32) - low.astype(F32)).astype(BF16)
    new = lax.broadcasted_iota(jnp.int32, (width, width), 0)
    old = lax.broadcasted_iota(jnp.int32, (width, width), 1)
    wanted = jnp.where(new < width // 2, 2 * new, 2 * new - width + 1)
    pick = jnp.where(old == wanted, 1.0, 0.0).astype(BF16)
    rows = jnp.dot(pick, jnp.concatenate([high, low, rest], axis=1), preferred_element_type=F32)
    old = lax.broadcasted_iota(jnp.int32, (width, width), 0)
    new = lax.broadcasted_iota(jnp.int32, (width, width), 1)
    wanted = jnp.where(new < width // 2, 2 * new, 2 * new - width + 1)
    pick = jnp.where(old == wanted, 1.0, 0.0).astype(BF16)
    return jnp.dot(
        rows.astype(BF16), jnp.concatenate([pick, pick, pick], axis=0), preferred_element_type=F32
    )


def place(shape, coords, slot, row=0):
    rows = lax.broadcasted_iota(jnp.int32, shape, 0) + row
    columns = lax.broadcasted_iota(jnp.int32, shape, 1)
    return rows >= coords[0, slot], columns >= coords[1, slot]


def window(region, coords, slot):
    rows, columns = place(region.shape[2:], coords, slot)
    return [
        jnp.where(
            columns,
            jnp.where(rows, region[plane, 0], region[plane, 2]),
            jnp.where(rows, region[plane, 1], region[plane, 3]),
        )
        for plane in range(2)
    ]


def deposit(source, totals, first, coords):
    width = totals.shape[-1]
    tall = 32

    @pl.loop(0, width // tall)
    def _(piece):
        at = pl.ds(pl.multiple_of(piece * tall, tall), tall)
        sums = None
        for slot in range(coords.shape[1]):
            rows, columns = place((tall, width), coords, slot, piece * tall)
            parts = []
            for value in source(slot, at):
                left, right = jnp.where(columns, value, 0.0), jnp.where(columns, 0.0, value)
                for side, mask in ((left, rows), (right, rows)):
                    parts.append(jnp.where(mask, side, 0.0))
                for side, mask in ((left, rows), (right, rows)):
                    parts.append(jnp.where(mask, 0.0, side))
            sums = parts if sums is None else [a + b for a, b in zip(sums, parts)]
        for index, total in enumerate(sums):
            totals[first + index // 4, index % 4, at] = total


def stage(count, source, between, after, tables, hook):
    forth, back = tables
    spectra = to_spectrum([source(slot) for slot in range(count)], *forth)
    hook(0)
    moved = [between(slot, *pair) for slot, pair in enumerate(spectra)]
    outs = from_spectrum(moved, *back)
    hook(1)
    for slot, pair in enumerate(outs):
        after(slot, *pair)


def kernel(coords, live, own, probe_in, phase_in, amplitude_in, left_in, right_in, *refs):
    updated, one, two, twice, phase, amplitude, left_t, right_t, probe, wave, back, *refs = refs
    inverse, totals, passing, got, local, gates, *sems = refs
    width = own.shape[-1]
    count = coords.shape[1]
    has, where = neighbours()
    greet(has, where)
    links = Links(sems)
    halo = Halo(own, (one, two), links, has, where)
    sums = Sums(totals, passing, got, links, has, where)
    pieces = range(CHUNKS)
    row = lax.axis_index("ty")
    even = lax.rem(row, 2) == 0
    odd = jnp.logical_not(even)

    def across(planes):
        for plane in planes:
            for piece in pieces:
                halo.across[plane, piece].start()

    def down(planes):
        for plane in planes:
            for piece in pieces:
                halo.down[plane, piece].start()

    def forward(planes):
        for plane in planes:
            for piece in pieces:
                halo.forward(plane, piece)

    def hand(at, step):
        @pl.when((row + step >= 0) & (row + step < lax.axis_size("ty")))
        def _():
            pl.semaphore_signal(
                gates.at[at],
                inc=1,
                device_id={"ty": row + step},
                device_id_type=pl.DeviceIdType.MESH,
            )

    pl.when(even)(lambda: across([0, 1]))
    down([0, 1])
    fetches = [
        pltpu.make_async_copy(source, target, local.at[at])
        for at, (source, target) in enumerate(
            [
                (probe_in, twice.at[:, slice(0, width)]),
                (probe_in, twice.at[:, slice(width, 2 * width)]),
                (phase_in, phase.at[0]),
                (amplitude_in, amplitude),
                (left_in, left_t),
                (right_in, right_t),
                (own.at[0:2], one.at[:, 0]),
                (own.at[2:4], two.at[:, 0]),
            ]
        )
    ]
    for fetch in fetches:
        fetch.start()
    for fetch in fetches[:2]:
        fetch.wait()

    @pl.loop(0, count)
    def _(slot):
        top, left = coords[0, slot], coords[1, slot]
        alive = jnp.minimum(jnp.maximum(live[0] - slot, 0), 1).astype(F32)
        start = width - top
        for plane in range(2):
            rows = twice[plane, pl.ds((start >> 3) * 8, width + 8), :]
            rows = pltpu.roll(rows, lax.rem(width + 8 - (start & 7), width + 8), 0)[:width]
            probe[slot, plane] = pltpu.roll(rows, left, 1) * alive

    def power(of):
        def source(slot, rows):
            real, imag = of[slot, 0, rows], of[slot, 1, rows]
            return [real * real + imag * imag]

        return source

    def crossed(of, by):
        def source(slot, rows):
            real, imag = by[slot, 0, rows], by[slot, 1, rows]
            first, second = of[slot, 0, rows], of[slot, 1, rows]
            return [first * real + second * imag, first * imag - second * real]

        return source

    deposit(power(probe), totals, 0, coords)
    sums.start([0])
    halo.blank(one)
    halo.blank(two)
    fetches[2].wait()
    cosine, sine = turn_of(phase[0])
    phase[0], phase[1] = even_odd(cosine), even_odd(sine)
    fetches[3].wait()

    @pl.loop(0, count)
    def _(slot):
        amplitude[slot] = even_odd(amplitude[slot])

    @pl.when(even)
    def _():
        forward([0])
        halo.across[1, 0].sent()
        hand(0, 1)
        forward([1])
        down([2, 3])

    @pl.when(odd)
    def _():
        pl.semaphore_wait(gates.at[0], 1)
        across([0, 1])

    for piece in pieces:
        sums.turn(0, piece)
    for fetch in fetches[4:]:
        fetch.wait()

    @pl.when(odd)
    def _():
        forward([0])
        halo.across[1, 0].sent()
        hand(1, -1)
        forward([1])
        down([2, 3])

    @pl.when(even)
    def _():
        pl.when(has["down"])(lambda: pl.semaphore_wait(gates.at[1], 1))
        across([2, 3])

    halo.finish([0, 1])
    forth = [left_t.at[0], left_t.at[1]], [right_t.at[0], right_t.at[1]]
    tables = forth, ([left_t.at[2], left_t.at[3]], [right_t.at[2], right_t.at[3]])

    def first_source(slot):
        real, imag = window(one, coords, slot)
        probe_r, probe_i = probe[slot, 0], probe[slot, 1]
        return probe_r * real - probe_i * imag, probe_r * imag + probe_i * real

    def first_between(slot, real, imag):
        return real * phase[0] - imag * phase[1], real * phase[1] + imag * phase[0]

    def keep(target):
        def after(slot, real, imag):
            target[slot, 0], target[slot, 1] = real, imag

        return after

    def nothing(spot):
        pass

    def share(spot):
        if spot == 0:

            @pl.when(even)
            def _():
                halo.across[2, 0].sent()
                hand(2, 1)

            @pl.when(odd)
            def _():
                pl.semaphore_wait(gates.at[2], 1)
                across([2, 3])

        else:
            pl.when(even)(lambda: forward([2]))

    stage(count, first_source, first_between, keep(wave), tables, share)
    deposit(power(wave), totals, 1, coords)
    sums.start([1])
    pl.when(even)(lambda: forward([3]))
    for piece in pieces:
        sums.turn(1, piece)
    pl.when(odd)(lambda: forward([2, 3]))
    halo.finish([2, 3])

    def second_source(slot):
        second_r, second_i = window(two, coords, slot)
        wave_r, wave_i = wave[slot, 0], wave[slot, 1]
        return wave_r * second_r - wave_i * second_i, wave_r * second_i + wave_i * second_r

    def second_between(slot, real, imag):
        size = jnp.minimum(lax.rsqrt(real * real + imag * imag), 2.0)
        ratio = amplitude[slot] * size - 1.0
        return real * ratio, imag * ratio

    stage(count, second_source, second_between, keep(back), tables, nothing)
    deposit(crossed(wave, back), totals, 2, coords)
    sums.start([2, 3])

    def third_source(slot):
        second_r, second_i = window(two, coords, slot)
        real, imag = back[slot, 0], back[slot, 1]
        return second_r * real + second_i * imag, second_r * imag - second_i * real

    def third_between(slot, real, imag):
        return real * phase[0] + imag * phase[1], imag * phase[0] - real * phase[1]

    def turn(planes):
        for plane in planes:
            for piece in pieces:
                sums.turn(plane, piece)

    far = even & has["up"]
    near = jnp.logical_not(far)
    pl.when(near)(lambda: turn([2, 3]))

    def turn_far(spot):
        pl.when(far)(lambda: turn([2 + spot]))

    stage(count, third_source, third_between, keep(back), tables, turn_far)
    deposit(crossed(probe, back), totals, 4, coords)
    sums.start([4, 5])
    turn([4, 5])
    sums.finish([0, 1, 2, 3])
    inverse[...] = 1.0 / (sums.total(0) + 1.0)
    for plane in range(2):
        updated[2 + plane] = two[plane, 0] + sums.total(2 + plane) / (sums.total(1) + 1.0)
    sums.finish([4, 5])
    for plane in range(2):
        updated[plane] = one[plane, 0] + sums.total(4 + plane) * inverse[...]
    pl.when(odd)(halo.across[2, 0].sent)
    links.sent([halo.across[1, 0], halo.across[2, 0]])


def on_device(object_planes, probe, phase, coords, live, amplitude):
    width = probe.shape[-1]
    slots = coords.shape[2]
    left_t, right_t = dft_tables(width)
    smem = pl.BlockSpec(memory_space=pltpu.SMEM)
    hbm = pl.BlockSpec(memory_space=pltpu.HBM)
    vmem = pl.BlockSpec(memory_space=pltpu.VMEM)

    def scratch(*shape):
        return pltpu.VMEM((*shape, width, width), F32)

    links = 4 * 3 * CHUNKS + 6 * (2 * CHUNKS + 1)

    return pl.pallas_call(
        kernel,
        out_shape=jax.ShapeDtypeStruct(object_planes.shape, F32),
        in_specs=[smem] * 2 + [hbm] * 6,
        out_specs=vmem,
        scratch_shapes=[
            scratch(2, 4),
            scratch(2, 4),
            pltpu.VMEM((2, 2 * width + 8, width), F32),
            scratch(2),
            scratch(slots),
            pltpu.VMEM(left_t.shape, BF16),
            pltpu.VMEM(right_t.shape, BF16),
            scratch(slots, 2),
            scratch(slots, 2),
            scratch(slots, 2),
            scratch(),
            scratch(6, 4),
            scratch(6),
            scratch(3, 6),
            pltpu.SemaphoreType.DMA((8,)),
            pltpu.SemaphoreType.REGULAR((3,)),
            pltpu.SemaphoreType.DMA((links,)),
            pltpu.SemaphoreType.DMA((links,)),
        ],
        compiler_params=pltpu.CompilerParams(
            vmem_limit_bytes=60 << 20, collective_id=0, has_side_effects=True
        ),
        cost_estimate=pl.CostEstimate(
            flops=48 * slots * width**3, bytes_accessed=8 << 20, transcendentals=0
        ),
        name="iteration",
    )(coords[0, 0].T, live[0], object_planes, probe, phase, amplitude[0, 0], left_t, right_t)


def solution(mesh):
    return jax.shard_map(
        on_device,
        mesh=mesh,
        in_specs=(
            P(None, ("groups", "ty"), "tx"),
            P(),
            P(),
            P(("groups", "ty"), "tx", None, None),
            P(("groups", "ty"), "tx"),
            P(("groups", "ty"), "tx", None, None, None),
        ),
        out_specs=P(None, ("groups", "ty"), "tx"),
        check_vma=False,
    )
```

```python
import math

import jax
import jax.numpy as jnp
import numpy as np
from jax import lax
from jax.experimental import pallas as pl
from jax.experimental.pallas import tpu as pltpu
from jax.sharding import PartitionSpec as P

F32 = jnp.float32
BF16 = jnp.bfloat16
CHUNKS = 2


def dft_tables(width):
    half = width // 2
    scale = 1.0 / math.sqrt(width)

    def stacked(table, axis):
        table = table.astype(np.float32)
        high = table.astype(BF16)
        low = (table - high.astype(np.float32)).astype(BF16)
        return np.concatenate([high, high, low], axis=axis)

    lefts, rights = [], []
    for parity in range(2):
        index = (2 * np.arange(half) + parity)[:, None] * np.arange(half)[None, :] % width
        angles = index * (2.0 * math.pi / width)
        real, imag = np.cos(angles) * scale, -np.sin(angles) * scale
        whole = np.block([[real, -imag], [imag, real]])
        lefts.append((stacked(whole, 1), stacked(whole.T, 1)))
        rights.append((stacked(whole.T, 0), stacked(whole, 0)))
    left = np.stack([lefts[parity][way] for way in range(2) for parity in range(2)])
    right = np.stack([rights[parity][way] for way in range(2) for parity in range(2)])
    return jnp.asarray(left), jnp.asarray(right)


def split(value):
    high = value.astype(BF16)
    low = (value - high.astype(F32)).astype(BF16)
    return high, low


def tripled(value, axis):
    high, low = split(value)
    return jnp.concatenate([high, low, high], axis=axis)


def to_spectrum(values, left, right):
    width = values[0][0].shape[0]
    half = width // 2
    sides = []
    for parity in range(2):
        columns = []
        for pair in values:
            parts = [v[:half] - v[half:] if parity else v[:half] + v[half:] for v in pair]
            columns.append(tripled(jnp.concatenate(parts, axis=0), 0))
        data = jnp.concatenate(columns, axis=1)
        sides.append(jnp.dot(left[parity][...], data, preferred_element_type=F32))
    outs = []
    for parity in range(2):
        rows = []
        for at in range(len(values)):
            cut = slice(at * width, (at + 1) * width)
            parts = []
            for part in (slice(0, half), slice(half, width)):
                v = jnp.concatenate([sides[0][part, cut], sides[1][part, cut]], axis=0)
                parts.append(v[:, :half] - v[:, half:] if parity else v[:, :half] + v[:, half:])
            rows.append(tripled(jnp.concatenate(parts, axis=1), 1))
        data = jnp.concatenate(rows, axis=0)
        outs.append(jnp.dot(data, right[parity][...], preferred_element_type=F32))
    result = []
    for at in range(len(values)):
        rows = slice(at * width, (at + 1) * width)
        real = jnp.concatenate([outs[0][rows, :half], outs[1][rows, :half]], axis=1)
        imag = jnp.concatenate([outs[0][rows, half:], outs[1][rows, half:]], axis=1)
        result.append((real, imag))
    return result


def from_spectrum(values, left, right):
    width = values[0][0].shape[0]
    half = width // 2
    halves = (slice(0, half), slice(half, width))
    sides = []
    for parity in range(2):
        columns = []
        for pair in values:
            parts = [v[halves[parity]] for v in pair]
            columns.append(tripled(jnp.concatenate(parts, axis=0), 0))
        data = jnp.concatenate(columns, axis=1)
        sides.append(jnp.dot(left[parity][...], data, preferred_element_type=F32))
    tops = sides[0] + sides[1]
    lows = sides[0] - sides[1]
    outs = []
    for parity in range(2):
        rows = []
        for at in range(len(values)):
            cut = slice(at * width + parity * half, at * width + (parity + 1) * half)
            parts = [
                jnp.concatenate([tops[part, cut], lows[part, cut]], axis=0) for part in halves
            ]
            rows.append(tripled(jnp.concatenate(parts, axis=1), 1))
        data = jnp.concatenate(rows, axis=0)
        outs.append(jnp.dot(data, right[parity][...], preferred_element_type=F32))
    total, gap = outs[0] + outs[1], outs[0] - outs[1]
    result = []
    for at in range(len(values)):
        rows = slice(at * width, (at + 1) * width)
        real = jnp.concatenate([total[rows, :half], gap[rows, :half]], axis=1)
        imag = jnp.concatenate([total[rows, half:], gap[rows, half:]], axis=1)
        result.append((real, imag))
    return result


def rows_to_spectrum(values, right):
    tall, width = values[0][0].shape
    half = width // 2
    outs = []
    for parity in range(2):
        rows = []
        for pair in values:
            parts = [
                v[:, :half] - v[:, half:] if parity else v[:, :half] + v[:, half:] for v in pair
            ]
            rows.append(tripled(jnp.concatenate(parts, axis=1), 1))
        data = jnp.concatenate(rows, axis=0)
        outs.append(jnp.dot(data, right[parity][...], preferred_element_type=F32))
    result = []
    for at in range(len(values)):
        rows = slice(at * tall, (at + 1) * tall)
        result.append(
            [
                jnp.concatenate([outs[0][rows, part], outs[1][rows, part]], axis=1)
                for part in (slice(0, half), slice(half, width))
            ]
        )
    return result


def columns_to_spectrum(tops, lows, left):
    half, width = tops[0][0].shape
    sides = []
    for parity in range(2):
        columns = []
        for top, low in zip(tops, lows):
            parts = [t - b if parity else t + b for t, b in zip(top, low)]
            columns.append(tripled(jnp.concatenate(parts, axis=0), 0))
        data = jnp.concatenate(columns, axis=1)
        sides.append(jnp.dot(left[parity][...], data, preferred_element_type=F32))
    result = []
    for at in range(len(tops)):
        cut = slice(at * width, (at + 1) * width)
        result.append(
            [
                jnp.concatenate([sides[0][part, cut], sides[1][part, cut]], axis=0)
                for part in (slice(0, half), slice(half, width))
            ]
        )
    return result


def columns_from_spectrum(values, left):
    width = values[0][0].shape[0]
    half = width // 2
    halves = (slice(0, half), slice(half, width))
    sides = []
    for parity in range(2):
        columns = []
        for pair in values:
            parts = [v[halves[parity]] for v in pair]
            columns.append(tripled(jnp.concatenate(parts, axis=0), 0))
        data = jnp.concatenate(columns, axis=1)
        sides.append(jnp.dot(left[parity][...], data, preferred_element_type=F32))
    sets = []
    for both in (sides[0] + sides[1], sides[0] - sides[1]):
        cuts = [slice(at * width, (at + 1) * width) for at in range(len(values))]
        sets.append([[both[part, cut] for part in halves] for cut in cuts])
    return sets


def rows_from_spectrum(values, right):
    tall, width = values[0][0].shape
    half = width // 2
    halves = (slice(0, half), slice(half, width))
    outs = []
    for parity in range(2):
        rows = []
        for pair in values:
            parts = [v[:, halves[parity]] for v in pair]
            rows.append(tripled(jnp.concatenate(parts, axis=1), 1))
        data = jnp.concatenate(rows, axis=0)
        outs.append(jnp.dot(data, right[parity][...], preferred_element_type=F32))
    total, gap = outs[0] + outs[1], outs[0] - outs[1]
    result = []
    for at in range(len(values)):
        rows = slice(at * tall, (at + 1) * tall)
        result.append(
            [jnp.concatenate([total[rows, part], gap[rows, part]], axis=1) for part in halves]
        )
    return result


def neighbours():
    row, column = lax.axis_index("ty"), lax.axis_index("tx")
    has = {
        "up": row > 0,
        "down": row < lax.axis_size("ty") - 1,
        "left": column > 0,
        "right": column < lax.axis_size("tx") - 1,
    }
    where = {
        "up": {"ty": row - 1},
        "down": {"ty": row + 1},
        "left": {"tx": column - 1},
        "right": {"tx": column + 1},
    }
    return has, where


def greet(has, where):
    barrier = pltpu.get_barrier_semaphore()
    for side, there in has.items():

        @pl.when(there)
        def _():
            pl.semaphore_signal(
                barrier, inc=1, device_id=where[side], device_id_type=pl.DeviceIdType.MESH
            )

    peers = sum(there.astype(jnp.int32) for there in has.values())
    pl.semaphore_wait(barrier, peers)


class Links:
    def __init__(self, sems):
        self.sems, self.every = sems, []

    def link(self, source, target, device, sends, receives):
        at = len(self.every)
        made = Link(source, target, self.sems, at, device, sends, receives)
        self.every.append(made)
        return made

    def sent(self, but):
        for made in self.every:
            if made not in but:
                made.sent()


class Link:
    def __init__(self, source, target, sems, at, device, sends, receives):
        self.copy = pltpu.make_async_remote_copy(
            src_ref=source,
            dst_ref=target,
            send_sem=sems[0].at[at],
            recv_sem=sems[1].at[at],
            device_id=device,
            device_id_type=pl.DeviceIdType.MESH,
        )
        self.sends, self.receives = sends, receives

    def start(self):
        pl.when(self.sends)(self.copy.start)

    def sent(self):
        pl.when(self.sends)(self.copy.wait_send)

    def arrived(self):
        pl.when(self.receives)(self.copy.wait_recv)


class Halo:
    def __init__(self, own, regions, links, has, where):
        planes, width = own.shape[0], own.shape[-1]
        tall = width // CHUNKS
        forwards = has["up"] & has["right"], has["down"] & has["right"]
        self.has = has
        self.across, self.down, self.corner = {}, {}, {}
        for plane in range(planes):
            for piece in range(CHUNKS):
                rows = slice(piece * tall, (piece + 1) * tall)
                mine = own.at[plane, rows]
                right, below, diagonal = [
                    regions[plane // 2].at[plane % 2, quarter, rows] for quarter in (1, 2, 3)
                ]
                key = plane, piece
                self.across[key] = links.link(
                    mine, right, where["left"], has["left"], has["right"]
                )
                self.down[key] = links.link(mine, below, where["up"], has["up"], has["down"])
                self.corner[key] = links.link(right, diagonal, where["up"], *forwards)

    def blank(self, region):
        has = self.has
        zeros = jnp.zeros(region.shape[2:], F32)
        there = has["right"], has["down"], has["down"] & has["right"]
        for plane in range(2):
            for quarter in (1, 2, 3):

                @pl.when(jnp.logical_not(there[quarter - 1]))
                def _():
                    region[plane, quarter] = zeros

    def forward(self, plane, piece):
        self.across[plane, piece].arrived()
        self.corner[plane, piece].start()

    def finish(self, keys):
        for key in keys:
            self.down[key].arrived()
            self.corner[key].arrived()


class Sums:
    def __init__(self, totals, passing, got, links, has, where):
        self.totals, self.passing, self.got, self.has = totals, passing, got, has
        planes, width = passing.shape[0], passing.shape[-1]
        tall = width // CHUNKS
        self.corner, self.down, self.across = {}, {}, {}
        for plane in range(planes):
            for piece in range(CHUNKS):
                rows = slice(piece * tall, (piece + 1) * tall)
                self.corner[plane, piece] = links.link(
                    totals.at[plane, 3, rows],
                    got.at[0, plane, rows],
                    where["down"],
                    has["down"],
                    has["up"],
                )
                self.across[plane, piece] = links.link(
                    passing.at[plane, rows],
                    got.at[2, plane, rows],
                    where["right"],
                    has["right"],
                    has["left"],
                )
            self.down[plane] = links.link(
                totals.at[plane, 2], got.at[1, plane], where["down"], has["down"], has["up"]
            )

    def start(self, planes, pieces=range(CHUNKS)):
        for piece in pieces:
            for plane in planes:
                self.corner[plane, piece].start()
        if CHUNKS - 1 in pieces:
            for plane in planes:
                self.down[plane].start()

    def turn(self, plane, piece):
        tall = self.passing.shape[-1] // CHUNKS
        rows = slice(piece * tall, (piece + 1) * tall)
        self.corner[plane, piece].arrived()
        came = jnp.where(self.has["up"], self.got[0, plane, rows], 0.0)
        self.passing[plane, rows] = self.totals[plane, 1, rows] + came
        self.across[plane, piece].start()

    def finish(self, planes):
        for plane in planes:
            self.down[plane].arrived()
            for piece in range(CHUNKS):
                self.across[plane, piece].arrived()

    def total(self, plane):
        above = jnp.where(self.has["up"], self.got[1, plane], 0.0)
        beside = jnp.where(self.has["left"], self.got[2, plane], 0.0)
        return self.totals[plane, 0] + above + beside


def turn_of(phase):
    half = phase * 0.5
    square = half * half
    for at in range(7, -1, -1):
        sign = -1.0 if at % 2 else 1.0
        if at == 7:
            cosine, sine = sign * (1.0 / math.factorial(14)), sign * (1.0 / math.factorial(15))
        else:
            cosine = cosine * square + sign / math.factorial(2 * at)
            sine = sine * square + sign / math.factorial(2 * at + 1)
    sine = sine * half
    return 1.0 - 2.0 * sine * sine, 2.0 * sine * cosine


def even_odd(value):
    width = value.shape[0]
    high, low = split(value)
    rest = (value - high.astype(F32) - low.astype(F32)).astype(BF16)
    new = lax.broadcasted_iota(jnp.int32, (width, width), 0)
    old = lax.broadcasted_iota(jnp.int32, (width, width), 1)
    wanted = jnp.where(new < width // 2, 2 * new, 2 * new - width + 1)
    pick = jnp.where(old == wanted, 1.0, 0.0).astype(BF16)
    rows = jnp.dot(pick, jnp.concatenate([high, low, rest], axis=1), preferred_element_type=F32)
    old = lax.broadcasted_iota(jnp.int32, (width, width), 0)
    new = lax.broadcasted_iota(jnp.int32, (width, width), 1)
    wanted = jnp.where(new < width // 2, 2 * new, 2 * new - width + 1)
    pick = jnp.where(old == wanted, 1.0, 0.0).astype(BF16)
    return jnp.dot(
        rows.astype(BF16), jnp.concatenate([pick, pick, pick], axis=0), preferred_element_type=F32
    )


def place(shape, coords, slot, row=0):
    rows = lax.broadcasted_iota(jnp.int32, shape, 0) + row
    columns = lax.broadcasted_iota(jnp.int32, shape, 1)
    return rows >= coords[0, slot], columns >= coords[1, slot]


def window(region, coords, slot, start=0, stop=None):
    width = region.shape[-1]
    stop = stop or width
    at = slice(start, stop)
    rows, columns = place((stop - start, width), coords, slot, start)
    return [
        jnp.where(
            columns,
            jnp.where(rows, region[plane, 0, at], region[plane, 2, at]),
            jnp.where(rows, region[plane, 1, at], region[plane, 3, at]),
        )
        for plane in range(2)
    ]


def deposit(source, totals, first, coords, part=(0, 1)):
    width = totals.shape[-1]
    tall = 32

    first_row, last_row = [width * bound // part[1] for bound in (part[0], part[0] + 1)]

    @pl.loop(first_row // tall, last_row // tall)
    def _(piece):
        at = pl.ds(pl.multiple_of(piece * tall, tall), tall)
        sums = None
        for slot in range(coords.shape[1]):
            rows, columns = place((tall, width), coords, slot, piece * tall)
            parts = []
            for value in source(slot, at):
                left, right = jnp.where(columns, value, 0.0), jnp.where(columns, 0.0, value)
                for side, mask in ((left, rows), (right, rows)):
                    parts.append(jnp.where(mask, side, 0.0))
                for side, mask in ((left, rows), (right, rows)):
                    parts.append(jnp.where(mask, 0.0, side))
            sums = parts if sums is None else [a + b for a, b in zip(sums, parts)]
        for index, total in enumerate(sums):
            totals[first + index // 4, index % 4, at] = total


def stage(count, source, between, after, tables, hook):
    forth, back = tables
    spectra = to_spectrum([source(slot) for slot in range(count)], *forth)
    hook(0)
    moved = [between(slot, *pair) for slot, pair in enumerate(spectra)]
    outs = from_spectrum(moved, *back)
    hook(1)
    for slot, pair in enumerate(outs):
        after(slot, *pair)


def kernel(coords, live, own, probe_in, phase_in, amplitude_in, left_in, right_in, *refs):
    updated, one, two, twice, phase, amplitude, left_t, right_t, probe, wave, back, *refs = refs
    inverse, totals, passing, got, local, gates, *sems = refs
    width = own.shape[-1]
    count = coords.shape[1]
    has, where = neighbours()
    greet(has, where)
    links = Links(sems)
    halo = Halo(own, (one, two), links, has, where)
    sums = Sums(totals, passing, got, links, has, where)
    pieces = range(CHUNKS)
    row = lax.axis_index("ty")
    even = lax.rem(row, 2) == 0
    odd = jnp.logical_not(even)

    ones = [(plane, piece) for plane in (0, 1) for piece in pieces]
    upper, lower = [[(plane, piece) for plane in (2, 3)] for piece in pieces]

    def across(keys):
        for key in keys:
            halo.across[key].start()

    def down(keys):
        for key in keys:
            halo.down[key].start()

    def forward(keys):
        for key in keys:
            halo.forward(*key)

    def hand(at, step):
        @pl.when((row + step >= 0) & (row + step < lax.axis_size("ty")))
        def _():
            pl.semaphore_signal(
                gates.at[at],
                inc=1,
                device_id={"ty": row + step},
                device_id_type=pl.DeviceIdType.MESH,
            )

    pl.when(even)(lambda: across(ones))
    down(ones)
    fetches = [
        pltpu.make_async_copy(source, target, local.at[at])
        for at, (source, target) in enumerate(
            [
                (probe_in, twice.at[:, slice(0, width)]),
                (probe_in, twice.at[:, slice(width, 2 * width)]),
                (phase_in, phase.at[0]),
                (amplitude_in, amplitude),
                (left_in, left_t),
                (right_in, right_t),
                (own.at[0:2], one.at[:, 0]),
                (own.at[2:4], two.at[:, 0]),
            ]
        )
    ]
    for fetch in fetches:
        fetch.start()
    for fetch in fetches[:2]:
        fetch.wait()

    @pl.loop(0, count)
    def _(slot):
        top, left = coords[0, slot], coords[1, slot]
        alive = jnp.minimum(jnp.maximum(live[0] - slot, 0), 1).astype(F32)
        start = width - top
        for plane in range(2):
            rows = twice[plane, pl.ds((start >> 3) * 8, width + 8), :]
            rows = pltpu.roll(rows, lax.rem(width + 8 - (start & 7), width + 8), 0)[:width]
            probe[slot, plane] = pltpu.roll(rows, left, 1) * alive

    def power(of):
        def source(slot, rows):
            real, imag = of[slot, 0, rows], of[slot, 1, rows]
            return [real * real + imag * imag]

        return source

    def crossed(of, by):
        def source(slot, rows):
            real, imag = by[slot, 0, rows], by[slot, 1, rows]
            first, second = of[slot, 0, rows], of[slot, 1, rows]
            return [first * real + second * imag, first * imag - second * real]

        return source

    deposit(power(probe), totals, 0, coords)
    sums.start([0])
    halo.blank(one)
    halo.blank(two)
    fetches[2].wait()
    cosine, sine = turn_of(phase[0])
    phase[0], phase[1] = even_odd(cosine), even_odd(sine)
    fetches[3].wait()

    @pl.loop(0, count)
    def _(slot):
        amplitude[slot] = even_odd(amplitude[slot])

    @pl.when(even)
    def _():
        forward(ones[:CHUNKS])
        halo.across[1, 0].sent()
        hand(0, 1)
        forward(ones[CHUNKS:])
        down(upper + lower)

    @pl.when(odd)
    def _():
        pl.semaphore_wait(gates.at[0], 1)
        across(ones)

    for piece in pieces:
        sums.turn(0, piece)
    for fetch in fetches[4:]:
        fetch.wait()

    @pl.when(odd)
    def _():
        forward(ones[:CHUNKS])
        halo.across[1, 0].sent()
        hand(1, -1)
        forward(ones[CHUNKS:])
        down(upper + lower)

    @pl.when(even)
    def _():
        pl.when(has["down"])(lambda: pl.semaphore_wait(gates.at[1], 1))
        across(upper + lower)

    halo.finish(ones)
    forth = [left_t.at[0], left_t.at[1]], [right_t.at[0], right_t.at[1]]
    tables = forth, ([left_t.at[2], left_t.at[3]], [right_t.at[2], right_t.at[3]])

    def first_source(slot):
        real, imag = window(one, coords, slot)
        probe_r, probe_i = probe[slot, 0], probe[slot, 1]
        return probe_r * real - probe_i * imag, probe_r * imag + probe_i * real

    def first_between(slot, real, imag):
        return real * phase[0] - imag * phase[1], real * phase[1] + imag * phase[0]

    def keep(target):
        def after(slot, real, imag):
            target[slot, 0], target[slot, 1] = real, imag

        return after

    def nothing(spot):
        pass

    def share(spot):
        if spot == 0:

            @pl.when(even)
            def _():
                halo.across[2, 0].sent()
                hand(2, 1)

            @pl.when(odd)
            def _():
                pl.semaphore_wait(gates.at[2], 1)
                across(upper + lower)

        else:
            pl.when(even)(lambda: forward(upper))

    stage(count, first_source, first_between, keep(wave), tables, share)
    deposit(power(wave), totals, 1, coords)
    sums.start([1])
    pl.when(even)(lambda: forward(lower))
    for piece in pieces:
        sums.turn(1, piece)
    pl.when(odd)(lambda: forward(upper))
    half = width // 2
    left_f, right_f = tables[0]
    left_b, right_b = tables[1]

    def exits(start):
        values = []
        for slot in range(count):
            second_r, second_i = window(two, coords, slot, start, start + half)
            wave_r, wave_i = [wave[slot, part, slice(start, start + half)] for part in range(2)]
            values.append(
                (wave_r * second_r - wave_i * second_i, wave_r * second_i + wave_i * second_r)
            )
        return rows_to_spectrum(values, right_f)

    def second_between(slot, real, imag):
        size = jnp.minimum(lax.rsqrt(real * real + imag * imag), 2.0)
        ratio = amplitude[slot] * size - 1.0
        return real * ratio, imag * ratio

    def turn(planes, pieces=pieces):
        for plane in planes:
            for piece in pieces:
                sums.turn(plane, piece)

    halo.finish(upper)
    tops = exits(0)
    pl.when(odd)(lambda: forward(lower))
    halo.finish(lower)
    lows = exits(half)
    far = columns_to_spectrum(tops, lows, left_f)
    moved = [second_between(slot, *pair) for slot, pair in enumerate(far)]
    sets = columns_from_spectrum(moved, left_b)
    for piece, values in enumerate(sets):
        for slot, pair in enumerate(rows_from_spectrum(values, right_b)):
            for part in range(2):
                back[slot, part, slice(piece * half, (piece + 1) * half)] = pair[part]
        deposit(crossed(wave, back), totals, 2, coords, (piece, CHUNKS))
        sums.start([2, 3], [piece])
        if piece == 0:
            pl.when(jnp.logical_not(has["up"]))(lambda: turn([2, 3], [0]))

    def third_source(slot):
        second_r, second_i = window(two, coords, slot)
        real, imag = back[slot, 0], back[slot, 1]
        return second_r * real + second_i * imag, second_r * imag - second_i * real

    def third_between(slot, real, imag):
        return real * phase[0] + imag * phase[1], imag * phase[0] - real * phase[1]

    far = even & has["up"]
    pl.when(jnp.logical_not(has["up"]))(lambda: turn([2, 3], [1]))
    pl.when(odd)(lambda: turn([2, 3]))

    def turn_far(spot):
        pl.when(far)(lambda: turn([2 + spot]))

    stage(count, third_source, third_between, keep(back), tables, turn_far)
    deposit(crossed(probe, back), totals, 4, coords)
    sums.start([4, 5])
    turn([4, 5])
    sums.finish([0, 1, 2, 3])
    inverse[...] = 1.0 / (sums.total(0) + 1.0)
    for plane in range(2):
        updated[2 + plane] = two[plane, 0] + sums.total(2 + plane) / (sums.total(1) + 1.0)
    sums.finish([4, 5])
    for plane in range(2):
        updated[plane] = one[plane, 0] + sums.total(4 + plane) * inverse[...]
    pl.when(odd)(halo.across[2, 0].sent)
    links.sent([halo.across[1, 0], halo.across[2, 0]])


def on_device(object_planes, probe, phase, coords, live, amplitude):
    width = probe.shape[-1]
    slots = coords.shape[2]
    left_t, right_t = dft_tables(width)
    smem = pl.BlockSpec(memory_space=pltpu.SMEM)
    hbm = pl.BlockSpec(memory_space=pltpu.HBM)
    vmem = pl.BlockSpec(memory_space=pltpu.VMEM)

    def scratch(*shape):
        return pltpu.VMEM((*shape, width, width), F32)

    links = 4 * 3 * CHUNKS + 6 * (2 * CHUNKS + 1)

    return pl.pallas_call(
        kernel,
        out_shape=jax.ShapeDtypeStruct(object_planes.shape, F32),
        in_specs=[smem] * 2 + [hbm] * 6,
        out_specs=vmem,
        scratch_shapes=[
            scratch(2, 4),
            scratch(2, 4),
            pltpu.VMEM((2, 2 * width + 8, width), F32),
            scratch(2),
            scratch(slots),
            pltpu.VMEM(left_t.shape, BF16),
            pltpu.VMEM(right_t.shape, BF16),
            scratch(slots, 2),
            scratch(slots, 2),
            scratch(slots, 2),
            scratch(),
            scratch(6, 4),
            scratch(6),
            scratch(3, 6),
            pltpu.SemaphoreType.DMA((8,)),
            pltpu.SemaphoreType.REGULAR((3,)),
            pltpu.SemaphoreType.DMA((links,)),
            pltpu.SemaphoreType.DMA((links,)),
        ],
        compiler_params=pltpu.CompilerParams(
            vmem_limit_bytes=60 << 20, collective_id=0, has_side_effects=True
        ),
        cost_estimate=pl.CostEstimate(
            flops=48 * slots * width**3, bytes_accessed=8 << 20, transcendentals=0
        ),
        name="iteration",
    )(coords[0, 0].T, live[0], object_planes, probe, phase, amplitude[0, 0], left_t, right_t)


def solution(mesh):
    return jax.shard_map(
        on_device,
        mesh=mesh,
        in_specs=(
            P(None, ("groups", "ty"), "tx"),
            P(),
            P(),
            P(("groups", "ty"), "tx", None, None),
            P(("groups", "ty"), "tx"),
            P(("groups", "ty"), "tx", None, None, None),
        ),
        out_specs=P(None, ("groups", "ty"), "tx"),
        check_vma=False,
    )
```

```python
import math

import jax
import jax.numpy as jnp
import numpy as np
from jax import lax
from jax.experimental import pallas as pl
from jax.experimental.pallas import tpu as pltpu
from jax.sharding import PartitionSpec as P

F32 = jnp.float32
BF16 = jnp.bfloat16
HALVES = ((0, 2), (2, 4))
HALO_ROWS = (HALVES, HALVES, ((0, 2), (2, 3), (3, 4)), ((0, 2), (2, 3), (3, 4)))
EARLY = ((0, 1), (1, 2), (2, 4))
SUM_ROWS = (((0, 4),), ((0, 4),), EARLY, EARLY, HALVES, HALVES)


def rows_of(piece, width):
    return slice(piece[0] * width // 4, piece[1] * width // 4)


def dft_tables(width):
    half = width // 2
    scale = 1.0 / math.sqrt(width)

    def stacked(table, axis):
        table = table.astype(np.float32)
        high = table.astype(BF16)
        low = (table - high.astype(np.float32)).astype(BF16)
        return np.concatenate([high, high, low], axis=axis)

    lefts, rights = [], []
    for parity in range(2):
        index = (2 * np.arange(half) + parity)[:, None] * np.arange(half)[None, :] % width
        angles = index * (2.0 * math.pi / width)
        real, imag = np.cos(angles) * scale, -np.sin(angles) * scale
        whole = np.block([[real, -imag], [imag, real]])
        early = np.arange(width) % half < half // 2
        forth = [stacked(whole[:, columns], 1) for columns in (early, ~early)]
        lefts.append((np.concatenate(forth, axis=1), stacked(whole.T, 1)))
        rights.append((stacked(whole.T, 0), stacked(whole, 0)))
    left = np.stack([lefts[parity][way] for way in range(2) for parity in range(2)])
    right = np.stack([rights[parity][way] for way in range(2) for parity in range(2)])
    return jnp.asarray(left), jnp.asarray(right)


def split(value):
    high = value.astype(BF16)
    low = (value - high.astype(F32)).astype(BF16)
    return high, low


def tripled(value, axis):
    high, low = split(value)
    return jnp.concatenate([high, low, high], axis=axis)


def by_depth(parts):
    at = parts[0].shape[0] // 2
    return [
        tripled(jnp.concatenate([v[cut] for v in parts], axis=0), 0)
        for cut in (slice(0, at), slice(at, 2 * at))
    ]


def to_spectrum(values, left, right):
    width = values[0][0].shape[0]
    half = width // 2
    sides = []
    for parity in range(2):
        columns = []
        for pair in values:
            parts = [v[:half] - v[half:] if parity else v[:half] + v[half:] for v in pair]
            columns.append(jnp.concatenate(by_depth(parts), axis=0))
        data = jnp.concatenate(columns, axis=1)
        sides.append(jnp.dot(left[parity][...], data, preferred_element_type=F32))
    outs = []
    for parity in range(2):
        rows = []
        for at in range(len(values)):
            cut = slice(at * width, (at + 1) * width)
            parts = []
            for part in (slice(0, half), slice(half, width)):
                v = jnp.concatenate([sides[0][part, cut], sides[1][part, cut]], axis=0)
                parts.append(v[:, :half] - v[:, half:] if parity else v[:, :half] + v[:, half:])
            rows.append(tripled(jnp.concatenate(parts, axis=1), 1))
        data = jnp.concatenate(rows, axis=0)
        outs.append(jnp.dot(data, right[parity][...], preferred_element_type=F32))
    result = []
    for at in range(len(values)):
        rows = slice(at * width, (at + 1) * width)
        real = jnp.concatenate([outs[0][rows, :half], outs[1][rows, :half]], axis=1)
        imag = jnp.concatenate([outs[0][rows, half:], outs[1][rows, half:]], axis=1)
        result.append((real, imag))
    return result


def from_spectrum(values, left, right):
    width = values[0][0].shape[0]
    half = width // 2
    halves = (slice(0, half), slice(half, width))
    sides = []
    for parity in range(2):
        columns = []
        for pair in values:
            parts = [v[halves[parity]] for v in pair]
            columns.append(tripled(jnp.concatenate(parts, axis=0), 0))
        data = jnp.concatenate(columns, axis=1)
        sides.append(jnp.dot(left[parity][...], data, preferred_element_type=F32))
    tops = sides[0] + sides[1]
    lows = sides[0] - sides[1]
    outs = []
    for parity in range(2):
        rows = []
        for at in range(len(values)):
            cut = slice(at * width + parity * half, at * width + (parity + 1) * half)
            parts = [
                jnp.concatenate([tops[part, cut], lows[part, cut]], axis=0) for part in halves
            ]
            rows.append(tripled(jnp.concatenate(parts, axis=1), 1))
        data = jnp.concatenate(rows, axis=0)
        outs.append(jnp.dot(data, right[parity][...], preferred_element_type=F32))
    total, gap = outs[0] + outs[1], outs[0] - outs[1]
    result = []
    for at in range(len(values)):
        rows = slice(at * width, (at + 1) * width)
        real = jnp.concatenate([total[rows, :half], gap[rows, :half]], axis=1)
        imag = jnp.concatenate([total[rows, half:], gap[rows, half:]], axis=1)
        result.append((real, imag))
    return result


def rows_to_spectrum(values, right):
    tall, width = values[0][0].shape
    half = width // 2
    outs = []
    for parity in range(2):
        rows = []
        for pair in values:
            parts = [
                v[:, :half] - v[:, half:] if parity else v[:, :half] + v[:, half:] for v in pair
            ]
            rows.append(tripled(jnp.concatenate(parts, axis=1), 1))
        data = jnp.concatenate(rows, axis=0)
        outs.append(jnp.dot(data, right[parity][...], preferred_element_type=F32))
    result = []
    for at in range(len(values)):
        rows = slice(at * tall, (at + 1) * tall)
        result.append(
            [
                jnp.concatenate([outs[0][rows, part], outs[1][rows, part]], axis=1)
                for part in (slice(0, half), slice(half, width))
            ]
        )
    return result


def columns_part(tops, lows, left, cut):
    sides = []
    for parity in range(2):
        columns = []
        for top, low in zip(tops, lows):
            parts = [t - b if parity else t + b for t, b in zip(top, low)]
            columns.append(tripled(jnp.concatenate(parts, axis=0), 0))
        data = jnp.concatenate(columns, axis=1)
        sides.append(jnp.dot(left[parity][:, cut], data, preferred_element_type=F32))
    return sides


def columns_to_spectrum(early, late, count):
    sides = [a + b for a, b in zip(early, late)]
    width = sides[0].shape[0]
    half = width // 2
    result = []
    for at in range(count):
        cut = slice(at * width, (at + 1) * width)
        result.append(
            [
                jnp.concatenate([sides[0][part, cut], sides[1][part, cut]], axis=0)
                for part in (slice(0, half), slice(half, width))
            ]
        )
    return result


def columns_from_spectrum(values, left):
    width = values[0][0].shape[0]
    half = width // 2
    halves = (slice(0, half), slice(half, width))
    sides = []
    for parity in range(2):
        columns = []
        for pair in values:
            parts = [v[halves[parity]] for v in pair]
            columns.append(tripled(jnp.concatenate(parts, axis=0), 0))
        data = jnp.concatenate(columns, axis=1)
        sides.append(jnp.dot(left[parity][...], data, preferred_element_type=F32))
    sets = []
    for both in (sides[0] + sides[1], sides[0] - sides[1]):
        cuts = [slice(at * width, (at + 1) * width) for at in range(len(values))]
        sets.append([[both[part, cut] for part in halves] for cut in cuts])
    return sets


def rows_from_spectrum(values, right):
    tall, width = values[0][0].shape
    half = width // 2
    halves = (slice(0, half), slice(half, width))
    outs = []
    for parity in range(2):
        rows = []
        for pair in values:
            parts = [v[:, halves[parity]] for v in pair]
            rows.append(tripled(jnp.concatenate(parts, axis=1), 1))
        data = jnp.concatenate(rows, axis=0)
        outs.append(jnp.dot(data, right[parity][...], preferred_element_type=F32))
    total, gap = outs[0] + outs[1], outs[0] - outs[1]
    result = []
    for at in range(len(values)):
        rows = slice(at * tall, (at + 1) * tall)
        result.append(
            [jnp.concatenate([total[rows, part], gap[rows, part]], axis=1) for part in halves]
        )
    return result


def neighbours():
    row, column = lax.axis_index("ty"), lax.axis_index("tx")
    has = {
        "up": row > 0,
        "down": row < lax.axis_size("ty") - 1,
        "left": column > 0,
        "right": column < lax.axis_size("tx") - 1,
    }
    where = {
        "up": {"ty": row - 1},
        "down": {"ty": row + 1},
        "left": {"tx": column - 1},
        "right": {"tx": column + 1},
    }
    return has, where


def greet(has, where):
    barrier = pltpu.get_barrier_semaphore()
    for side, there in has.items():

        @pl.when(there)
        def _():
            pl.semaphore_signal(
                barrier, inc=1, device_id=where[side], device_id_type=pl.DeviceIdType.MESH
            )

    peers = sum(there.astype(jnp.int32) for there in has.values())
    pl.semaphore_wait(barrier, peers)


class Links:
    def __init__(self, sems):
        self.sems, self.every = sems, []

    def link(self, source, target, device, sends, receives):
        at = len(self.every)
        made = Link(source, target, self.sems, at, device, sends, receives)
        self.every.append(made)
        return made

    def sent(self, but):
        for made in self.every:
            if made not in but:
                made.sent()


class Link:
    def __init__(self, source, target, sems, at, device, sends, receives):
        self.copy = pltpu.make_async_remote_copy(
            src_ref=source,
            dst_ref=target,
            send_sem=sems[0].at[at],
            recv_sem=sems[1].at[at],
            device_id=device,
            device_id_type=pl.DeviceIdType.MESH,
        )
        self.sends, self.receives = sends, receives

    def start(self):
        pl.when(self.sends)(self.copy.start)

    def sent(self):
        pl.when(self.sends)(self.copy.wait_send)

    def arrived(self):
        pl.when(self.receives)(self.copy.wait_recv)


class Halo:
    def __init__(self, own, regions, links, has, where):
        planes, width = own.shape[0], own.shape[-1]
        forwards = has["up"] & has["right"], has["down"] & has["right"]
        self.has = has
        self.across, self.down, self.corner = {}, {}, {}
        for plane in range(planes):
            for piece, cut in enumerate(HALO_ROWS[plane]):
                rows = rows_of(cut, width)
                mine = own.at[plane, rows]
                right, below, diagonal = [
                    regions[plane // 2].at[plane % 2, quarter, rows] for quarter in (1, 2, 3)
                ]
                key = plane, piece
                self.across[key] = links.link(
                    mine, right, where["left"], has["left"], has["right"]
                )
                self.down[key] = links.link(mine, below, where["up"], has["up"], has["down"])
                self.corner[key] = links.link(right, diagonal, where["up"], *forwards)

    def blank(self, region):
        has = self.has
        zeros = jnp.zeros(region.shape[2:], F32)
        there = has["right"], has["down"], has["down"] & has["right"]
        for plane in range(2):
            for quarter in (1, 2, 3):

                @pl.when(jnp.logical_not(there[quarter - 1]))
                def _():
                    region[plane, quarter] = zeros

    def forward(self, plane, piece):
        self.across[plane, piece].arrived()
        self.corner[plane, piece].start()

    def finish(self, keys):
        for key in keys:
            self.down[key].arrived()
            self.corner[key].arrived()


class Sums:
    def __init__(self, totals, passing, got, links, has, where):
        self.totals, self.passing, self.got, self.has = totals, passing, got, has
        planes, width = passing.shape[0], passing.shape[-1]
        self.corner, self.down, self.across = {}, {}, {}
        for plane in range(planes):
            for piece, cut in enumerate(SUM_ROWS[plane]):
                rows = rows_of(cut, width)
                self.corner[plane, piece] = links.link(
                    totals.at[plane, 3, rows],
                    got.at[0, plane, rows],
                    where["down"],
                    has["down"],
                    has["up"],
                )
                self.across[plane, piece] = links.link(
                    passing.at[plane, rows],
                    got.at[2, plane, rows],
                    where["right"],
                    has["right"],
                    has["left"],
                )
            self.down[plane] = links.link(
                totals.at[plane, 2], got.at[1, plane], where["down"], has["down"], has["up"]
            )

    def start(self, planes, pieces=None):
        last = len(SUM_ROWS[planes[0]]) - 1
        for piece in range(last + 1) if pieces is None else pieces:
            for plane in planes:
                self.corner[plane, piece].start()
            if piece == last:
                for plane in planes:
                    self.down[plane].start()

    def turn(self, planes, pieces=None):
        for piece in range(len(SUM_ROWS[planes[0]])) if pieces is None else pieces:
            for plane in planes:
                rows = rows_of(SUM_ROWS[plane][piece], self.passing.shape[-1])
                self.corner[plane, piece].arrived()
                came = jnp.where(self.has["up"], self.got[0, plane, rows], 0.0)
                self.passing[plane, rows] = self.totals[plane, 1, rows] + came
                self.across[plane, piece].start()

    def finish(self, planes):
        for plane in planes:
            self.down[plane].arrived()
            for piece in range(len(SUM_ROWS[plane])):
                self.across[plane, piece].arrived()

    def total(self, plane):
        above = jnp.where(self.has["up"], self.got[1, plane], 0.0)
        beside = jnp.where(self.has["left"], self.got[2, plane], 0.0)
        return self.totals[plane, 0] + above + beside


def turn_of(phase):
    half = phase * 0.5
    square = half * half
    for at in range(7, -1, -1):
        sign = -1.0 if at % 2 else 1.0
        if at == 7:
            cosine, sine = sign * (1.0 / math.factorial(14)), sign * (1.0 / math.factorial(15))
        else:
            cosine = cosine * square + sign / math.factorial(2 * at)
            sine = sine * square + sign / math.factorial(2 * at + 1)
    sine = sine * half
    return 1.0 - 2.0 * sine * sine, 2.0 * sine * cosine


def even_odd(value):
    width = value.shape[0]
    high, low = split(value)
    rest = (value - high.astype(F32) - low.astype(F32)).astype(BF16)
    new = lax.broadcasted_iota(jnp.int32, (width, width), 0)
    old = lax.broadcasted_iota(jnp.int32, (width, width), 1)
    wanted = jnp.where(new < width // 2, 2 * new, 2 * new - width + 1)
    pick = jnp.where(old == wanted, 1.0, 0.0).astype(BF16)
    rows = jnp.dot(pick, jnp.concatenate([high, low, rest], axis=1), preferred_element_type=F32)
    old = lax.broadcasted_iota(jnp.int32, (width, width), 0)
    new = lax.broadcasted_iota(jnp.int32, (width, width), 1)
    wanted = jnp.where(new < width // 2, 2 * new, 2 * new - width + 1)
    pick = jnp.where(old == wanted, 1.0, 0.0).astype(BF16)
    return jnp.dot(
        rows.astype(BF16), jnp.concatenate([pick, pick, pick], axis=0), preferred_element_type=F32
    )


def place(shape, coords, slot, row=0):
    rows = lax.broadcasted_iota(jnp.int32, shape, 0) + row
    columns = lax.broadcasted_iota(jnp.int32, shape, 1)
    return rows >= coords[0, slot], columns >= coords[1, slot]


def window(region, coords, slot, start=0, stop=None):
    width = region.shape[-1]
    stop = stop or width
    at = slice(start, stop)
    rows, columns = place((stop - start, width), coords, slot, start)
    return [
        jnp.where(
            columns,
            jnp.where(rows, region[plane, 0, at], region[plane, 2, at]),
            jnp.where(rows, region[plane, 1, at], region[plane, 3, at]),
        )
        for plane in range(2)
    ]


def deposit(source, totals, first, coords, part=(0, 4)):
    width = totals.shape[-1]
    tall = 32

    first_row, last_row = [width * bound // 4 for bound in part]

    @pl.loop(first_row // tall, last_row // tall)
    def _(piece):
        at = pl.ds(pl.multiple_of(piece * tall, tall), tall)
        sums = None
        for slot in range(coords.shape[1]):
            rows, columns = place((tall, width), coords, slot, piece * tall)
            parts = []
            for value in source(slot, at):
                left, right = jnp.where(columns, value, 0.0), jnp.where(columns, 0.0, value)
                for side, mask in ((left, rows), (right, rows)):
                    parts.append(jnp.where(mask, side, 0.0))
                for side, mask in ((left, rows), (right, rows)):
                    parts.append(jnp.where(mask, 0.0, side))
            sums = parts if sums is None else [a + b for a, b in zip(sums, parts)]
        for index, total in enumerate(sums):
            totals[first + index // 4, index % 4, at] = total


def stage(count, source, between, after, tables, hook):
    forth, back = tables
    spectra = to_spectrum([source(slot) for slot in range(count)], *forth)
    hook(0)
    moved = [between(slot, *pair) for slot, pair in enumerate(spectra)]
    outs = from_spectrum(moved, *back)
    hook(1)
    for slot, pair in enumerate(outs):
        after(slot, *pair)


def kernel(coords, live, own, probe_in, phase_in, amplitude_in, left_in, right_in, *refs):
    out, updated, one, two, twice, phase, amplitude, left_t, right_t, probe, wave, back, *refs = refs
    inverse, totals, passing, got, local, parting, gates, *sems = refs
    width = own.shape[-1]
    count = coords.shape[1]
    has, where = neighbours()
    greet(has, where)
    links = Links(sems)
    halo = Halo(own, (one, two), links, has, where)
    sums = Sums(totals, passing, got, links, has, where)
    row = lax.axis_index("ty")
    even = lax.rem(row, 2) == 0
    odd = jnp.logical_not(even)

    ones = [(plane, piece) for plane in (0, 1) for piece in range(len(HALVES))]
    twos = [[(plane, piece) for plane in (2, 3)] for piece in range(len(HALO_ROWS[2]))]
    all_twos = sum(twos, [])

    def across(keys):
        for key in keys:
            halo.across[key].start()

    def down(keys):
        for key in keys:
            halo.down[key].start()

    def forward(keys):
        for key in keys:
            halo.forward(*key)

    def hand(at, step):
        @pl.when((row + step >= 0) & (row + step < lax.axis_size("ty")))
        def _():
            pl.semaphore_signal(
                gates.at[at],
                inc=1,
                device_id={"ty": row + step},
                device_id_type=pl.DeviceIdType.MESH,
            )

    pl.when(even)(lambda: across(ones))
    down(ones)
    fetches = [
        pltpu.make_async_copy(source, target, local.at[at])
        for at, (source, target) in enumerate(
            [
                (probe_in, twice.at[:, slice(0, width)]),
                (probe_in, twice.at[:, slice(width, 2 * width)]),
                (phase_in, phase.at[0]),
                (amplitude_in, amplitude),
                (left_in, left_t),
                (right_in, right_t),
                (own.at[0:2], one.at[:, 0]),
                (own.at[2:4], two.at[:, 0]),
            ]
        )
    ]
    for fetch in fetches:
        fetch.start()
    for fetch in fetches[:2]:
        fetch.wait()

    @pl.loop(0, count)
    def _(slot):
        top, left = coords[0, slot], coords[1, slot]
        alive = jnp.minimum(jnp.maximum(live[0] - slot, 0), 1).astype(F32)
        start = width - top
        for plane in range(2):
            rows = twice[plane, pl.ds((start >> 3) * 8, width + 8), :]
            rows = pltpu.roll(rows, lax.rem(width + 8 - (start & 7), width + 8), 0)[:width]
            probe[slot, plane] = pltpu.roll(rows, left, 1) * alive

    def power(of):
        def source(slot, rows):
            real, imag = of[slot, 0, rows], of[slot, 1, rows]
            return [real * real + imag * imag]

        return source

    def crossed(of, by):
        def source(slot, rows):
            real, imag = by[slot, 0, rows], by[slot, 1, rows]
            first, second = of[slot, 0, rows], of[slot, 1, rows]
            return [first * real + second * imag, first * imag - second * real]

        return source

    deposit(power(probe), totals, 0, coords)
    sums.start([0])
    halo.blank(one)
    halo.blank(two)
    fetches[2].wait()
    cosine, sine = turn_of(phase[0])
    phase[0], phase[1] = even_odd(cosine), even_odd(sine)
    fetches[3].wait()

    @pl.loop(0, count)
    def _(slot):
        amplitude[slot] = even_odd(amplitude[slot])

    @pl.when(even)
    def _():
        forward(ones[: len(HALVES)])
        halo.across[1, 0].sent()
        hand(0, 1)
        forward(ones[len(HALVES) :])
        down(all_twos)

    @pl.when(odd)
    def _():
        pl.semaphore_wait(gates.at[0], 1)
        across(ones)

    sums.turn([0])
    for fetch in fetches[4:]:
        fetch.wait()

    @pl.when(odd)
    def _():
        forward(ones[: len(HALVES)])
        halo.across[1, 0].sent()
        hand(1, -1)
        forward(ones[len(HALVES) :])
        down(all_twos)

    @pl.when(even)
    def _():
        pl.when(has["down"])(lambda: pl.semaphore_wait(gates.at[1], 1))
        across(all_twos)

    halo.finish(ones)
    forth = [left_t.at[0], left_t.at[1]], [right_t.at[0], right_t.at[1]]
    tables = forth, ([left_t.at[2], left_t.at[3]], [right_t.at[2], right_t.at[3]])

    def first_source(slot):
        real, imag = window(one, coords, slot)
        probe_r, probe_i = probe[slot, 0], probe[slot, 1]
        return probe_r * real - probe_i * imag, probe_r * imag + probe_i * real

    def first_between(slot, real, imag):
        return real * phase[0] - imag * phase[1], real * phase[1] + imag * phase[0]

    def keep(target):
        def after(slot, real, imag):
            target[slot, 0], target[slot, 1] = real, imag

        return after

    def nothing(spot):
        pass

    @pl.when(even)
    def _():
        halo.across[2, 0].sent()
        hand(2, 1)

    @pl.when(odd)
    def _():
        pl.semaphore_wait(gates.at[2], 1)
        across(all_twos)

    def share(spot):
        pl.when(even)(lambda: forward(twos[spot]))

    stage(count, first_source, first_between, keep(wave), tables, share)
    deposit(power(wave), totals, 1, coords)
    sums.start([1])
    pl.when(even)(lambda: forward(twos[2]))
    sums.turn([1])
    half, tall = width // 2, width // 4
    left_f, right_f = tables[0]
    left_b, right_b = tables[1]

    def exits(piece):
        at = rows_of(piece, width)
        values = []
        for slot in range(count):
            second_r, second_i = window(two, coords, slot, at.start, at.stop)
            wave_r, wave_i = [wave[slot, part, at] for part in range(2)]
            values.append(
                (wave_r * second_r - wave_i * second_i, wave_r * second_i + wave_i * second_r)
            )
        return rows_to_spectrum(values, right_f)

    def second_between(slot, real, imag):
        size = jnp.minimum(lax.rsqrt(real * real + imag * imag), 2.0)
        ratio = amplitude[slot] * size - 1.0
        return real * ratio, imag * ratio

    rows, parts = [], []
    for piece, keys in enumerate(twos):
        pl.when(odd)(lambda: forward(keys))
        halo.finish(keys)
        rows.append(exits(HALO_ROWS[2][piece]))
        if piece > 0:
            at = (piece - 1) * tall
            tops = [[v[at : at + tall] for v in pair] for pair in rows[0]]
            depth = slice((piece - 1) * 6 * tall, piece * 6 * tall)
            parts.append(columns_part(tops, rows[piece], left_f, depth))
    far = columns_to_spectrum(*parts, count)
    moved = [second_between(slot, *pair) for slot, pair in enumerate(far)]
    sets = columns_from_spectrum(moved, left_b)
    for piece, cut in enumerate(EARLY):
        at = rows_of(cut, width)
        side = at.start // half
        inside = slice(at.start - side * half, at.stop - side * half)
        values = [[v[inside] for v in pair] for pair in sets[side]]
        for slot, pair in enumerate(rows_from_spectrum(values, right_b)):
            for part in range(2):
                back[slot, part, at] = pair[part]
        deposit(crossed(wave, back), totals, 2, coords, cut)
        sums.start([2, 3], [piece])
        pl.when(jnp.logical_not(has["up"]))(lambda: sums.turn([2, 3], [piece]))
        if piece > 0:
            pl.when(odd)(lambda: sums.turn([2, 3], [piece - 1]))

    def third_source(slot):
        second_r, second_i = window(two, coords, slot)
        real, imag = back[slot, 0], back[slot, 1]
        return second_r * real + second_i * imag, second_r * imag - second_i * real

    def third_between(slot, real, imag):
        return real * phase[0] + imag * phase[1], imag * phase[0] - real * phase[1]

    far = even & has["up"]
    pl.when(odd)(lambda: sums.turn([2, 3], [2]))

    def turn_far(spot):
        pl.when(far)(lambda: sums.turn([2, 3], [[0, 1], [2]][spot]))

    stage(count, third_source, third_between, keep(back), tables, turn_far)
    deposit(crossed(probe, back), totals, 4, coords)
    sums.start([4, 5])
    sums.turn([4, 5])
    sums.finish([0, 1, 2, 3])
    inverse[...] = 1.0 / (sums.total(0) + 1.0)
    leaving = [pltpu.make_async_copy(updated.at[at], out.at[at], parting.at[at]) for at in range(4)]
    for plane in range(2):
        updated[2 + plane] = two[plane, 0] + sums.total(2 + plane) / (sums.total(1) + 1.0)
        leaving[2 + plane].start()
    for plane in range(2):
        sums.finish([4 + plane])
        updated[plane] = one[plane, 0] + sums.total(4 + plane) * inverse[...]
        leaving[plane].start()
    pl.when(odd)(halo.across[2, 0].sent)
    for copy in leaving:
        copy.wait()
    links.sent([halo.across[1, 0], halo.across[2, 0]])


def on_device(object_planes, probe, phase, coords, live, amplitude):
    width = probe.shape[-1]
    slots = coords.shape[2]
    left_t, right_t = dft_tables(width)
    smem = pl.BlockSpec(memory_space=pltpu.SMEM)
    hbm = pl.BlockSpec(memory_space=pltpu.HBM)

    def scratch(*shape):
        return pltpu.VMEM((*shape, width, width), F32)

    links = sum(3 * len(cuts) for cuts in HALO_ROWS)
    links += sum(2 * len(cuts) + 1 for cuts in SUM_ROWS)

    return pl.pallas_call(
        kernel,
        out_shape=jax.ShapeDtypeStruct(object_planes.shape, F32),
        in_specs=[smem] * 2 + [hbm] * 6,
        out_specs=hbm,
        scratch_shapes=[
            scratch(4),
            scratch(2, 4),
            scratch(2, 4),
            pltpu.VMEM((2, 2 * width + 8, width), F32),
            scratch(2),
            scratch(slots),
            pltpu.VMEM(left_t.shape, BF16),
            pltpu.VMEM(right_t.shape, BF16),
            scratch(slots, 2),
            scratch(slots, 2),
            scratch(slots, 2),
            scratch(),
            scratch(6, 4),
            scratch(6),
            scratch(3, 6),
            pltpu.SemaphoreType.DMA((8,)),
            pltpu.SemaphoreType.DMA((4,)),
            pltpu.SemaphoreType.REGULAR((3,)),
            pltpu.SemaphoreType.DMA((links,)),
            pltpu.SemaphoreType.DMA((links,)),
        ],
        compiler_params=pltpu.CompilerParams(
            vmem_limit_bytes=60 << 20, collective_id=0, has_side_effects=True
        ),
        cost_estimate=pl.CostEstimate(
            flops=48 * slots * width**3, bytes_accessed=8 << 20, transcendentals=0
        ),
        name="iteration",
    )(coords[0, 0].T, live[0], object_planes, probe, phase, amplitude[0, 0], left_t, right_t)


def solution(mesh):
    return jax.shard_map(
        on_device,
        mesh=mesh,
        in_specs=(
            P(None, ("groups", "ty"), "tx"),
            P(),
            P(),
            P(("groups", "ty"), "tx", None, None),
            P(("groups", "ty"), "tx"),
            P(("groups", "ty"), "tx", None, None, None),
        ),
        out_specs=P(None, ("groups", "ty"), "tx"),
        check_vma=False,
    )
```

```python
import math

import jax
import jax.numpy as jnp
import numpy as np
from jax import lax
from jax.experimental import pallas as pl
from jax.experimental.pallas import tpu as pltpu
from jax.sharding import PartitionSpec as P

F32 = jnp.float32
BF16 = jnp.bfloat16
HALVES = ((0, 2), (2, 4))
HALO_ROWS = (HALVES, HALVES, ((0, 2), (2, 3), (3, 4)), ((0, 2), (2, 3), (3, 4)))
EARLY = ((0, 1), (1, 2), (2, 4))
SUM_ROWS = (((0, 4),), ((0, 4),), EARLY, EARLY, HALVES, HALVES)


def rows_of(piece, width):
    return slice(piece[0] * width // 4, piece[1] * width // 4)


def dft_tables(width):
    half = width // 2
    scale = 1.0 / math.sqrt(width)

    def stacked(table, axis):
        table = table.astype(np.float32)
        high = table.astype(BF16)
        low = (table - high.astype(np.float32)).astype(BF16)
        return np.concatenate([high, high, low], axis=axis)

    lefts, rights = [], []
    for parity in range(2):
        index = (2 * np.arange(half) + parity)[:, None] * np.arange(half)[None, :] % width
        angles = index * (2.0 * math.pi / width)
        real, imag = np.cos(angles) * scale, -np.sin(angles) * scale
        whole = np.block([[real, -imag], [imag, real]])
        early = np.arange(width) % half < half // 2
        forth = [stacked(whole[:, columns], 1) for columns in (early, ~early)]
        lefts.append((np.concatenate(forth, axis=1), stacked(whole.T, 1)))
        rights.append((stacked(whole.T, 0), stacked(whole, 0)))
    left = np.stack([lefts[parity][way] for way in range(2) for parity in range(2)])
    right = np.stack([rights[parity][way] for way in range(2) for parity in range(2)])
    return jnp.asarray(left), jnp.asarray(right)


def split(value):
    high = value.astype(BF16)
    low = (value - high.astype(F32)).astype(BF16)
    return high, low


def tripled(value, axis):
    high, low = split(value)
    return jnp.concatenate([high, low, high], axis=axis)


def by_depth(parts):
    at = parts[0].shape[0] // 2
    return [
        tripled(jnp.concatenate([v[cut] for v in parts], axis=0), 0)
        for cut in (slice(0, at), slice(at, 2 * at))
    ]


def to_spectrum(values, left, right):
    width = values[0][0].shape[0]
    half = width // 2
    sides = []
    for parity in range(2):
        columns = []
        for pair in values:
            parts = [v[:half] - v[half:] if parity else v[:half] + v[half:] for v in pair]
            columns.append(jnp.concatenate(by_depth(parts), axis=0))
        data = jnp.concatenate(columns, axis=1)
        sides.append(jnp.dot(left[parity][...], data, preferred_element_type=F32))
    outs = []
    for parity in range(2):
        rows = []
        for at in range(len(values)):
            cut = slice(at * width, (at + 1) * width)
            parts = []
            for part in (slice(0, half), slice(half, width)):
                v = jnp.concatenate([sides[0][part, cut], sides[1][part, cut]], axis=0)
                parts.append(v[:, :half] - v[:, half:] if parity else v[:, :half] + v[:, half:])
            rows.append(tripled(jnp.concatenate(parts, axis=1), 1))
        data = jnp.concatenate(rows, axis=0)
        outs.append(jnp.dot(data, right[parity][...], preferred_element_type=F32))
    result = []
    for at in range(len(values)):
        rows = slice(at * width, (at + 1) * width)
        real = jnp.concatenate([outs[0][rows, :half], outs[1][rows, :half]], axis=1)
        imag = jnp.concatenate([outs[0][rows, half:], outs[1][rows, half:]], axis=1)
        result.append((real, imag))
    return result


def from_spectrum(values, left, right):
    width = values[0][0].shape[0]
    half = width // 2
    halves = (slice(0, half), slice(half, width))
    sides = []
    for parity in range(2):
        columns = []
        for pair in values:
            parts = [v[halves[parity]] for v in pair]
            columns.append(tripled(jnp.concatenate(parts, axis=0), 0))
        data = jnp.concatenate(columns, axis=1)
        sides.append(jnp.dot(left[parity][...], data, preferred_element_type=F32))
    tops = sides[0] + sides[1]
    lows = sides[0] - sides[1]
    outs = []
    for parity in range(2):
        rows = []
        for at in range(len(values)):
            cut = slice(at * width + parity * half, at * width + (parity + 1) * half)
            parts = [
                jnp.concatenate([tops[part, cut], lows[part, cut]], axis=0) for part in halves
            ]
            rows.append(tripled(jnp.concatenate(parts, axis=1), 1))
        data = jnp.concatenate(rows, axis=0)
        outs.append(jnp.dot(data, right[parity][...], preferred_element_type=F32))
    total, gap = outs[0] + outs[1], outs[0] - outs[1]
    result = []
    for at in range(len(values)):
        rows = slice(at * width, (at + 1) * width)
        real = jnp.concatenate([total[rows, :half], gap[rows, :half]], axis=1)
        imag = jnp.concatenate([total[rows, half:], gap[rows, half:]], axis=1)
        result.append((real, imag))
    return result


def rows_to_spectrum(values, right):
    tall, width = values[0][0].shape
    half = width // 2
    outs = []
    for parity in range(2):
        rows = []
        for pair in values:
            parts = [
                v[:, :half] - v[:, half:] if parity else v[:, :half] + v[:, half:] for v in pair
            ]
            rows.append(tripled(jnp.concatenate(parts, axis=1), 1))
        data = jnp.concatenate(rows, axis=0)
        outs.append(jnp.dot(data, right[parity][...], preferred_element_type=F32))
    result = []
    for at in range(len(values)):
        rows = slice(at * tall, (at + 1) * tall)
        result.append(
            [
                jnp.concatenate([outs[0][rows, part], outs[1][rows, part]], axis=1)
                for part in (slice(0, half), slice(half, width))
            ]
        )
    return result


def columns_part(tops, lows, left, cut):
    sides = []
    for parity in range(2):
        columns = []
        for top, low in zip(tops, lows):
            parts = [t - b if parity else t + b for t, b in zip(top, low)]
            columns.append(tripled(jnp.concatenate(parts, axis=0), 0))
        data = jnp.concatenate(columns, axis=1)
        sides.append(jnp.dot(left[parity][:, cut], data, preferred_element_type=F32))
    return sides


def columns_to_spectrum(early, late, count):
    sides = [a + b for a, b in zip(early, late)]
    width = sides[0].shape[0]
    half = width // 2
    result = []
    for at in range(count):
        cut = slice(at * width, (at + 1) * width)
        result.append(
            [
                jnp.concatenate([sides[0][part, cut], sides[1][part, cut]], axis=0)
                for part in (slice(0, half), slice(half, width))
            ]
        )
    return result


def columns_from_spectrum(values, left):
    width = values[0][0].shape[0]
    half = width // 2
    halves = (slice(0, half), slice(half, width))
    sides = []
    for parity in range(2):
        columns = []
        for pair in values:
            parts = [v[halves[parity]] for v in pair]
            columns.append(tripled(jnp.concatenate(parts, axis=0), 0))
        data = jnp.concatenate(columns, axis=1)
        sides.append(jnp.dot(left[parity][...], data, preferred_element_type=F32))
    sets = []
    for both in (sides[0] + sides[1], sides[0] - sides[1]):
        cuts = [slice(at * width, (at + 1) * width) for at in range(len(values))]
        sets.append([[both[part, cut] for part in halves] for cut in cuts])
    return sets


def rows_from_spectrum(values, right):
    tall, width = values[0][0].shape
    half = width // 2
    halves = (slice(0, half), slice(half, width))
    outs = []
    for parity in range(2):
        rows = []
        for pair in values:
            parts = [v[:, halves[parity]] for v in pair]
            rows.append(tripled(jnp.concatenate(parts, axis=1), 1))
        data = jnp.concatenate(rows, axis=0)
        outs.append(jnp.dot(data, right[parity][...], preferred_element_type=F32))
    total, gap = outs[0] + outs[1], outs[0] - outs[1]
    result = []
    for at in range(len(values)):
        rows = slice(at * tall, (at + 1) * tall)
        result.append(
            [jnp.concatenate([total[rows, part], gap[rows, part]], axis=1) for part in halves]
        )
    return result


def neighbours():
    row, column = lax.axis_index("ty"), lax.axis_index("tx")
    has = {
        "up": row > 0,
        "down": row < lax.axis_size("ty") - 1,
        "left": column > 0,
        "right": column < lax.axis_size("tx") - 1,
    }
    where = {
        "up": {"ty": row - 1},
        "down": {"ty": row + 1},
        "left": {"tx": column - 1},
        "right": {"tx": column + 1},
    }
    return has, where


def greet(has, where):
    barrier = pltpu.get_barrier_semaphore()
    for side, there in has.items():

        @pl.when(there)
        def _():
            pl.semaphore_signal(
                barrier, inc=1, device_id=where[side], device_id_type=pl.DeviceIdType.MESH
            )

    peers = sum(there.astype(jnp.int32) for there in has.values())
    pl.semaphore_wait(barrier, peers)


class Links:
    def __init__(self, sems):
        self.sems, self.every = sems, []

    def link(self, source, target, device, sends, receives):
        at = len(self.every)
        made = Link(source, target, self.sems, at, device, sends, receives)
        self.every.append(made)
        return made

    def sent(self, but):
        for made in self.every:
            if made not in but:
                made.sent()


class Link:
    def __init__(self, source, target, sems, at, device, sends, receives):
        self.copy = pltpu.make_async_remote_copy(
            src_ref=source,
            dst_ref=target,
            send_sem=sems[0].at[at],
            recv_sem=sems[1].at[at],
            device_id=device,
            device_id_type=pl.DeviceIdType.MESH,
        )
        self.sends, self.receives = sends, receives

    def start(self):
        pl.when(self.sends)(self.copy.start)

    def sent(self):
        pl.when(self.sends)(self.copy.wait_send)

    def arrived(self):
        pl.when(self.receives)(self.copy.wait_recv)


class Halo:
    def __init__(self, own, regions, links, has, where):
        planes, width = own.shape[0], own.shape[-1]
        forwards = has["up"] & has["right"], has["down"] & has["right"]
        self.has = has
        self.across, self.down, self.corner = {}, {}, {}
        for plane in range(planes):
            for piece, cut in enumerate(HALO_ROWS[plane]):
                rows = rows_of(cut, width)
                mine = own.at[plane, rows]
                right, below, diagonal = [
                    regions[plane // 2].at[plane % 2, quarter, rows] for quarter in (1, 2, 3)
                ]
                key = plane, piece
                self.across[key] = links.link(
                    mine, right, where["left"], has["left"], has["right"]
                )
                self.down[key] = links.link(mine, below, where["up"], has["up"], has["down"])
                self.corner[key] = links.link(right, diagonal, where["up"], *forwards)

    def blank(self, region):
        has = self.has
        zeros = jnp.zeros(region.shape[2:], F32)
        there = has["right"], has["down"], has["down"] & has["right"]
        for plane in range(2):
            for quarter in (1, 2, 3):

                @pl.when(jnp.logical_not(there[quarter - 1]))
                def _():
                    region[plane, quarter] = zeros

    def forward(self, plane, piece):
        self.across[plane, piece].arrived()
        self.corner[plane, piece].start()

    def finish(self, keys):
        for key in keys:
            self.down[key].arrived()
            self.corner[key].arrived()


class Sums:
    def __init__(self, totals, passing, got, links, has, where):
        self.totals, self.passing, self.got, self.has = totals, passing, got, has
        planes, width = passing.shape[0], passing.shape[-1]
        self.corner, self.down, self.across = {}, {}, {}
        for plane in range(planes):
            for piece, cut in enumerate(SUM_ROWS[plane]):
                rows = rows_of(cut, width)
                self.corner[plane, piece] = links.link(
                    totals.at[plane, 3, rows],
                    got.at[0, plane, rows],
                    where["down"],
                    has["down"],
                    has["up"],
                )
                self.across[plane, piece] = links.link(
                    passing.at[plane, rows],
                    got.at[2, plane, rows],
                    where["right"],
                    has["right"],
                    has["left"],
                )
            self.down[plane] = links.link(
                totals.at[plane, 2], got.at[1, plane], where["down"], has["down"], has["up"]
            )

    def start(self, planes, pieces=None):
        last = len(SUM_ROWS[planes[0]]) - 1
        for piece in range(last + 1) if pieces is None else pieces:
            for plane in planes:
                self.corner[plane, piece].start()
            if piece == last:
                for plane in planes:
                    self.down[plane].start()

    def turn(self, planes, pieces=None):
        for piece in range(len(SUM_ROWS[planes[0]])) if pieces is None else pieces:
            for plane in planes:
                rows = rows_of(SUM_ROWS[plane][piece], self.passing.shape[-1])
                self.corner[plane, piece].arrived()
                came = jnp.where(self.has["up"], self.got[0, plane, rows], 0.0)
                self.passing[plane, rows] = self.totals[plane, 1, rows] + came
                self.across[plane, piece].start()

    def finish(self, planes):
        for plane in planes:
            self.down[plane].arrived()
            for piece in range(len(SUM_ROWS[plane])):
                self.across[plane, piece].arrived()

    def total(self, plane):
        above = jnp.where(self.has["up"], self.got[1, plane], 0.0)
        beside = jnp.where(self.has["left"], self.got[2, plane], 0.0)
        return self.totals[plane, 0] + above + beside


def turn_of(phase):
    half = phase * 0.5
    square = half * half
    for at in range(7, -1, -1):
        sign = -1.0 if at % 2 else 1.0
        if at == 7:
            cosine, sine = sign * (1.0 / math.factorial(14)), sign * (1.0 / math.factorial(15))
        else:
            cosine = cosine * square + sign / math.factorial(2 * at)
            sine = sine * square + sign / math.factorial(2 * at + 1)
    sine = sine * half
    return 1.0 - 2.0 * sine * sine, 2.0 * sine * cosine


def even_odd(value):
    width = value.shape[0]
    high, low = split(value)
    rest = (value - high.astype(F32) - low.astype(F32)).astype(BF16)
    new = lax.broadcasted_iota(jnp.int32, (width, width), 0)
    old = lax.broadcasted_iota(jnp.int32, (width, width), 1)
    wanted = jnp.where(new < width // 2, 2 * new, 2 * new - width + 1)
    pick = jnp.where(old == wanted, 1.0, 0.0).astype(BF16)
    rows = jnp.dot(pick, jnp.concatenate([high, low, rest], axis=1), preferred_element_type=F32)
    old = lax.broadcasted_iota(jnp.int32, (width, width), 0)
    new = lax.broadcasted_iota(jnp.int32, (width, width), 1)
    wanted = jnp.where(new < width // 2, 2 * new, 2 * new - width + 1)
    pick = jnp.where(old == wanted, 1.0, 0.0).astype(BF16)
    return jnp.dot(
        rows.astype(BF16), jnp.concatenate([pick, pick, pick], axis=0), preferred_element_type=F32
    )


def place(shape, coords, slot, row=0):
    rows = lax.broadcasted_iota(jnp.int32, shape, 0) + row
    columns = lax.broadcasted_iota(jnp.int32, shape, 1)
    return rows >= coords[0, slot], columns >= coords[1, slot]


def window(region, coords, slot, start=0, stop=None):
    width = region.shape[-1]
    stop = stop or width
    at = slice(start, stop)
    rows, columns = place((stop - start, width), coords, slot, start)
    return [
        jnp.where(
            columns,
            jnp.where(rows, region[plane, 0, at], region[plane, 2, at]),
            jnp.where(rows, region[plane, 1, at], region[plane, 3, at]),
        )
        for plane in range(2)
    ]


def deposit(source, totals, first, coords, part=(0, 4)):
    width = totals.shape[-1]
    tall = 32

    first_row, last_row = [width * bound // 4 for bound in part]

    @pl.loop(first_row // tall, last_row // tall)
    def _(piece):
        at = pl.ds(pl.multiple_of(piece * tall, tall), tall)
        sums = None
        for slot in range(coords.shape[1]):
            rows, columns = place((tall, width), coords, slot, piece * tall)
            parts = []
            for value in source(slot, at):
                left, right = jnp.where(columns, value, 0.0), jnp.where(columns, 0.0, value)
                for side, mask in ((left, rows), (right, rows)):
                    parts.append(jnp.where(mask, side, 0.0))
                for side, mask in ((left, rows), (right, rows)):
                    parts.append(jnp.where(mask, 0.0, side))
            sums = parts if sums is None else [a + b for a, b in zip(sums, parts)]
        for index, total in enumerate(sums):
            totals[first + index // 4, index % 4, at] = total


def stage(count, source, between, after, tables, hook):
    forth, back = tables
    spectra = to_spectrum([source(slot) for slot in range(count)], *forth)
    hook(0)
    moved = [between(slot, *pair) for slot, pair in enumerate(spectra)]
    outs = from_spectrum(moved, *back)
    hook(1)
    for slot, pair in enumerate(outs):
        after(slot, *pair)


def kernel(coords, live, own, probe_in, phase_in, amplitude_in, left_in, right_in, *refs):
    out, updated, one, two, twice, phase, amplitude, left_t, right_t, probe, wave, back, *refs = refs
    inverse, totals, passing, got, local, parting, gates, *sems = refs
    width = own.shape[-1]
    count = coords.shape[1]
    has, where = neighbours()
    greet(has, where)
    links = Links(sems)
    halo = Halo(own, (one, two), links, has, where)
    sums = Sums(totals, passing, got, links, has, where)
    row = lax.axis_index("ty")
    even = lax.rem(row, 2) == 0
    odd = jnp.logical_not(even)

    ones = [(plane, piece) for plane in (0, 1) for piece in range(len(HALVES))]
    twos = [[(plane, piece) for plane in (2, 3)] for piece in range(len(HALO_ROWS[2]))]
    all_twos = sum(twos, [])

    def across(keys):
        for key in keys:
            halo.across[key].start()

    def down(keys):
        for key in keys:
            halo.down[key].start()

    def forward(keys):
        for key in keys:
            halo.forward(*key)

    def hand(at, step):
        @pl.when((row + step >= 0) & (row + step < lax.axis_size("ty")))
        def _():
            pl.semaphore_signal(
                gates.at[at],
                inc=1,
                device_id={"ty": row + step},
                device_id_type=pl.DeviceIdType.MESH,
            )

    pl.when(even)(lambda: across(ones))
    down(ones)
    fetches = [
        pltpu.make_async_copy(source, target, local.at[at])
        for at, (source, target) in enumerate(
            [
                (probe_in, twice.at[:, slice(0, width)]),
                (probe_in, twice.at[:, slice(width, 2 * width)]),
                (phase_in, phase.at[0]),
                (amplitude_in, amplitude),
                (left_in, left_t),
                (right_in, right_t),
                (own.at[0:2], one.at[:, 0]),
                (own.at[2:4], two.at[:, 0]),
            ]
        )
    ]
    for fetch in fetches:
        fetch.start()
    for fetch in fetches[:2]:
        fetch.wait()

    @pl.loop(0, count)
    def _(slot):
        top, left = coords[0, slot], coords[1, slot]
        alive = jnp.minimum(jnp.maximum(live[0] - slot, 0), 1).astype(F32)
        start = width - top
        for plane in range(2):
            rows = twice[plane, pl.ds((start >> 3) * 8, width + 8), :]
            rows = pltpu.roll(rows, lax.rem(width + 8 - (start & 7), width + 8), 0)[:width]
            probe[slot, plane] = pltpu.roll(rows, left, 1) * alive

    def power(of):
        def source(slot, rows):
            real, imag = of[slot, 0, rows], of[slot, 1, rows]
            return [real * real + imag * imag]

        return source

    def crossed(of, by):
        def source(slot, rows):
            real, imag = by[slot, 0, rows], by[slot, 1, rows]
            first, second = of[slot, 0, rows], of[slot, 1, rows]
            return [first * real + second * imag, first * imag - second * real]

        return source

    deposit(power(probe), totals, 0, coords)
    sums.start([0])
    halo.blank(one)
    halo.blank(two)

    @pl.when(even)
    def _():
        forward(ones[: len(HALVES)])
        halo.across[1, 0].sent()
        hand(0, 1)
        forward(ones[len(HALVES) :])
        down(all_twos)

    fetches[2].wait()
    cosine, sine = turn_of(phase[0])
    phase[0], phase[1] = even_odd(cosine), even_odd(sine)

    @pl.when(odd)
    def _():
        pl.semaphore_wait(gates.at[0], 1)
        across(ones)

    fetches[3].wait()

    @pl.loop(0, count)
    def _(slot):
        amplitude[slot] = even_odd(amplitude[slot])

    sums.turn([0])
    for fetch in fetches[4:]:
        fetch.wait()

    @pl.when(odd)
    def _():
        forward(ones[: len(HALVES)])
        halo.across[1, 0].sent()
        hand(1, -1)
        forward(ones[len(HALVES) :])
        down(all_twos)

    @pl.when(even)
    def _():
        pl.when(has["down"])(lambda: pl.semaphore_wait(gates.at[1], 1))
        across(all_twos)

    halo.finish(ones)
    forth = [left_t.at[0], left_t.at[1]], [right_t.at[0], right_t.at[1]]
    tables = forth, ([left_t.at[2], left_t.at[3]], [right_t.at[2], right_t.at[3]])

    def first_source(slot):
        real, imag = window(one, coords, slot)
        probe_r, probe_i = probe[slot, 0], probe[slot, 1]
        return probe_r * real - probe_i * imag, probe_r * imag + probe_i * real

    def first_between(slot, real, imag):
        return real * phase[0] - imag * phase[1], real * phase[1] + imag * phase[0]

    def keep(target):
        def after(slot, real, imag):
            target[slot, 0], target[slot, 1] = real, imag

        return after

    def nothing(spot):
        pass

    @pl.when(even)
    def _():
        halo.across[2, 0].sent()
        hand(2, 1)

    @pl.when(odd)
    def _():
        pl.semaphore_wait(gates.at[2], 1)
        across(all_twos)

    def share(spot):
        pl.when(even)(lambda: forward(twos[spot]))

    stage(count, first_source, first_between, keep(wave), tables, share)
    deposit(power(wave), totals, 1, coords)
    sums.start([1])
    pl.when(even)(lambda: forward(twos[2]))
    sums.turn([1])
    half, tall = width // 2, width // 4
    left_f, right_f = tables[0]
    left_b, right_b = tables[1]

    def exits(piece):
        at = rows_of(piece, width)
        values = []
        for slot in range(count):
            second_r, second_i = window(two, coords, slot, at.start, at.stop)
            wave_r, wave_i = [wave[slot, part, at] for part in range(2)]
            values.append(
                (wave_r * second_r - wave_i * second_i, wave_r * second_i + wave_i * second_r)
            )
        return rows_to_spectrum(values, right_f)

    def second_between(slot, real, imag):
        size = jnp.minimum(lax.rsqrt(real * real + imag * imag), 2.0)
        ratio = amplitude[slot] * size - 1.0
        return real * ratio, imag * ratio

    rows, parts = [], []
    for piece, keys in enumerate(twos):
        pl.when(odd)(lambda: forward(keys))
        halo.finish(keys)
        rows.append(exits(HALO_ROWS[2][piece]))
        if piece > 0:
            at = (piece - 1) * tall
            tops = [[v[at : at + tall] for v in pair] for pair in rows[0]]
            depth = slice((piece - 1) * 6 * tall, piece * 6 * tall)
            parts.append(columns_part(tops, rows[piece], left_f, depth))
    far = columns_to_spectrum(*parts, count)
    moved = [second_between(slot, *pair) for slot, pair in enumerate(far)]
    sets = columns_from_spectrum(moved, left_b)
    for piece, cut in enumerate(EARLY):
        at = rows_of(cut, width)
        side = at.start // half
        inside = slice(at.start - side * half, at.stop - side * half)
        values = [[v[inside] for v in pair] for pair in sets[side]]
        for slot, pair in enumerate(rows_from_spectrum(values, right_b)):
            for part in range(2):
                back[slot, part, at] = pair[part]
        deposit(crossed(wave, back), totals, 2, coords, cut)
        sums.start([2, 3], [piece])
        pl.when(jnp.logical_not(has["up"]))(lambda: sums.turn([2, 3], [piece]))
        if piece > 0:
            pl.when(odd)(lambda: sums.turn([2, 3], [piece - 1]))

    def third_source(slot):
        second_r, second_i = window(two, coords, slot)
        real, imag = back[slot, 0], back[slot, 1]
        return second_r * real + second_i * imag, second_r * imag - second_i * real

    def third_between(slot, real, imag):
        return real * phase[0] + imag * phase[1], imag * phase[0] - real * phase[1]

    far = even & has["up"]
    pl.when(odd)(lambda: sums.turn([2, 3], [2]))

    def turn_far(spot):
        pl.when(far)(lambda: sums.turn([2, 3], [[0, 1], [2]][spot]))

    stage(count, third_source, third_between, keep(back), tables, turn_far)
    deposit(crossed(probe, back), totals, 4, coords)
    sums.start([4, 5])
    sums.turn([4, 5])
    sums.finish([0, 1, 2, 3])
    inverse[...] = 1.0 / (sums.total(0) + 1.0)
    leaving = [pltpu.make_async_copy(updated.at[at], out.at[at], parting.at[at]) for at in range(4)]
    for plane in range(2):
        updated[2 + plane] = two[plane, 0] + sums.total(2 + plane) / (sums.total(1) + 1.0)
        leaving[2 + plane].start()
    for plane in range(2):
        sums.finish([4 + plane])
        updated[plane] = one[plane, 0] + sums.total(4 + plane) * inverse[...]
        leaving[plane].start()
    pl.when(odd)(halo.across[2, 0].sent)
    for copy in leaving:
        copy.wait()
    links.sent([halo.across[1, 0], halo.across[2, 0]])


def on_device(object_planes, probe, phase, coords, live, amplitude):
    width = probe.shape[-1]
    slots = coords.shape[2]
    left_t, right_t = dft_tables(width)
    smem = pl.BlockSpec(memory_space=pltpu.SMEM)
    hbm = pl.BlockSpec(memory_space=pltpu.HBM)

    def scratch(*shape):
        return pltpu.VMEM((*shape, width, width), F32)

    links = sum(3 * len(cuts) for cuts in HALO_ROWS)
    links += sum(2 * len(cuts) + 1 for cuts in SUM_ROWS)

    return pl.pallas_call(
        kernel,
        out_shape=jax.ShapeDtypeStruct(object_planes.shape, F32),
        in_specs=[smem] * 2 + [hbm] * 6,
        out_specs=hbm,
        scratch_shapes=[
            scratch(4),
            scratch(2, 4),
            scratch(2, 4),
            pltpu.VMEM((2, 2 * width + 8, width), F32),
            scratch(2),
            scratch(slots),
            pltpu.VMEM(left_t.shape, BF16),
            pltpu.VMEM(right_t.shape, BF16),
            scratch(slots, 2),
            scratch(slots, 2),
            scratch(slots, 2),
            scratch(),
            scratch(6, 4),
            scratch(6),
            scratch(3, 6),
            pltpu.SemaphoreType.DMA((8,)),
            pltpu.SemaphoreType.DMA((4,)),
            pltpu.SemaphoreType.REGULAR((3,)),
            pltpu.SemaphoreType.DMA((links,)),
            pltpu.SemaphoreType.DMA((links,)),
        ],
        compiler_params=pltpu.CompilerParams(
            vmem_limit_bytes=60 << 20, collective_id=0, has_side_effects=True
        ),
        cost_estimate=pl.CostEstimate(
            flops=48 * slots * width**3, bytes_accessed=8 << 20, transcendentals=0
        ),
        name="iteration",
    )(coords[0, 0].T, live[0], object_planes, probe, phase, amplitude[0, 0], left_t, right_t)


def solution(mesh):
    return jax.shard_map(
        on_device,
        mesh=mesh,
        in_specs=(
            P(None, ("groups", "ty"), "tx"),
            P(),
            P(),
            P(("groups", "ty"), "tx", None, None),
            P(("groups", "ty"), "tx"),
            P(("groups", "ty"), "tx", None, None, None),
        ),
        out_specs=P(None, ("groups", "ty"), "tx"),
        check_vma=False,
    )
```

```python
import math

import jax
import jax.numpy as jnp
import numpy as np
from jax import lax
from jax.experimental import pallas as pl
from jax.experimental.pallas import tpu as pltpu
from jax.sharding import PartitionSpec as P

F32 = jnp.float32
BF16 = jnp.bfloat16
HALVES = ((0, 2), (2, 4))
HALO_ROWS = (HALVES, HALVES, ((0, 2), (2, 3), (3, 4)), ((0, 2), (2, 3), (3, 4)))
EARLY = ((0, 1), (1, 2), (2, 4))
SUM_ROWS = (((0, 4),), ((0, 4),), EARLY, EARLY, HALVES, HALVES)


def rows_of(piece, width):
    return slice(piece[0] * width // 4, piece[1] * width // 4)


def dft_tables(width):
    half = width // 2
    scale = 1.0 / math.sqrt(width)

    def stacked(table, axis):
        table = table.astype(np.float32)
        high = table.astype(BF16)
        low = (table - high.astype(np.float32)).astype(BF16)
        return np.concatenate([high, high, low], axis=axis)

    lefts, rights = [], []
    for parity in range(2):
        index = (2 * np.arange(half) + parity)[:, None] * np.arange(half)[None, :] % width
        angles = index * (2.0 * math.pi / width)
        real, imag = np.cos(angles) * scale, -np.sin(angles) * scale
        whole = np.block([[real, -imag], [imag, real]])
        early = np.arange(width) % half < half // 2
        forth = [stacked(whole[:, columns], 1) for columns in (early, ~early)]
        lefts.append((np.concatenate(forth, axis=1), stacked(whole.T, 1)))
        rights.append((stacked(whole.T, 0), stacked(whole, 0)))
    left = np.stack([lefts[parity][way] for way in range(2) for parity in range(2)])
    right = np.stack([rights[parity][way] for way in range(2) for parity in range(2)])
    return jnp.asarray(left), jnp.asarray(right)


def split(value):
    high = value.astype(BF16)
    low = (value - high.astype(F32)).astype(BF16)
    return high, low


def tripled(value, axis):
    high, low = split(value)
    return jnp.concatenate([high, low, high], axis=axis)


def by_depth(parts):
    at = parts[0].shape[0] // 2
    return [
        tripled(jnp.concatenate([v[cut] for v in parts], axis=0), 0)
        for cut in (slice(0, at), slice(at, 2 * at))
    ]


def to_spectrum(values, left, right):
    width = values[0][0].shape[0]
    half = width // 2
    sides = []
    for parity in range(2):
        columns = []
        for pair in values:
            parts = [v[:half] - v[half:] if parity else v[:half] + v[half:] for v in pair]
            columns.append(jnp.concatenate(by_depth(parts), axis=0))
        data = jnp.concatenate(columns, axis=1)
        sides.append(jnp.dot(left[parity][...], data, preferred_element_type=F32))
    outs = []
    for parity in range(2):
        rows = []
        for at in range(len(values)):
            cut = slice(at * width, (at + 1) * width)
            parts = []
            for part in (slice(0, half), slice(half, width)):
                v = jnp.concatenate([sides[0][part, cut], sides[1][part, cut]], axis=0)
                parts.append(v[:, :half] - v[:, half:] if parity else v[:, :half] + v[:, half:])
            rows.append(tripled(jnp.concatenate(parts, axis=1), 1))
        data = jnp.concatenate(rows, axis=0)
        outs.append(jnp.dot(data, right[parity][...], preferred_element_type=F32))
    result = []
    for at in range(len(values)):
        rows = slice(at * width, (at + 1) * width)
        real = jnp.concatenate([outs[0][rows, :half], outs[1][rows, :half]], axis=1)
        imag = jnp.concatenate([outs[0][rows, half:], outs[1][rows, half:]], axis=1)
        result.append((real, imag))
    return result


def from_spectrum(values, left, right):
    width = values[0][0].shape[0]
    half = width // 2
    halves = (slice(0, half), slice(half, width))
    sides = []
    for parity in range(2):
        columns = []
        for pair in values:
            parts = [v[halves[parity]] for v in pair]
            columns.append(tripled(jnp.concatenate(parts, axis=0), 0))
        data = jnp.concatenate(columns, axis=1)
        sides.append(jnp.dot(left[parity][...], data, preferred_element_type=F32))
    tops = sides[0] + sides[1]
    lows = sides[0] - sides[1]
    outs = []
    for parity in range(2):
        rows = []
        for at in range(len(values)):
            cut = slice(at * width + parity * half, at * width + (parity + 1) * half)
            parts = [
                jnp.concatenate([tops[part, cut], lows[part, cut]], axis=0) for part in halves
            ]
            rows.append(tripled(jnp.concatenate(parts, axis=1), 1))
        data = jnp.concatenate(rows, axis=0)
        outs.append(jnp.dot(data, right[parity][...], preferred_element_type=F32))
    total, gap = outs[0] + outs[1], outs[0] - outs[1]
    result = []
    for at in range(len(values)):
        rows = slice(at * width, (at + 1) * width)
        real = jnp.concatenate([total[rows, :half], gap[rows, :half]], axis=1)
        imag = jnp.concatenate([total[rows, half:], gap[rows, half:]], axis=1)
        result.append((real, imag))
    return result


def rows_to_spectrum(values, right):
    tall, width = values[0][0].shape
    half = width // 2
    outs = []
    for parity in range(2):
        rows = []
        for pair in values:
            parts = [
                v[:, :half] - v[:, half:] if parity else v[:, :half] + v[:, half:] for v in pair
            ]
            rows.append(tripled(jnp.concatenate(parts, axis=1), 1))
        data = jnp.concatenate(rows, axis=0)
        outs.append(jnp.dot(data, right[parity][...], preferred_element_type=F32))
    result = []
    for at in range(len(values)):
        rows = slice(at * tall, (at + 1) * tall)
        result.append(
            [
                jnp.concatenate([outs[0][rows, part], outs[1][rows, part]], axis=1)
                for part in (slice(0, half), slice(half, width))
            ]
        )
    return result


def columns_part(tops, lows, left, cut):
    sides = []
    for parity in range(2):
        columns = []
        for top, low in zip(tops, lows):
            parts = [t - b if parity else t + b for t, b in zip(top, low)]
            columns.append(tripled(jnp.concatenate(parts, axis=0), 0))
        data = jnp.concatenate(columns, axis=1)
        sides.append(jnp.dot(left[parity][:, cut], data, preferred_element_type=F32))
    return sides


def columns_to_spectrum(early, late, count):
    sides = [a + b for a, b in zip(early, late)]
    width = sides[0].shape[0]
    half = width // 2
    result = []
    for at in range(count):
        cut = slice(at * width, (at + 1) * width)
        result.append(
            [
                jnp.concatenate([sides[0][part, cut], sides[1][part, cut]], axis=0)
                for part in (slice(0, half), slice(half, width))
            ]
        )
    return result


def columns_from_spectrum(values, left):
    width = values[0][0].shape[0]
    half = width // 2
    halves = (slice(0, half), slice(half, width))
    sides = []
    for parity in range(2):
        columns = []
        for pair in values:
            parts = [v[halves[parity]] for v in pair]
            columns.append(tripled(jnp.concatenate(parts, axis=0), 0))
        data = jnp.concatenate(columns, axis=1)
        sides.append(jnp.dot(left[parity][...], data, preferred_element_type=F32))
    sets = []
    for both in (sides[0] + sides[1], sides[0] - sides[1]):
        cuts = [slice(at * width, (at + 1) * width) for at in range(len(values))]
        sets.append([[both[part, cut] for part in halves] for cut in cuts])
    return sets


def rows_from_spectrum(values, right):
    tall, width = values[0][0].shape
    half = width // 2
    halves = (slice(0, half), slice(half, width))
    outs = []
    for parity in range(2):
        rows = []
        for pair in values:
            parts = [v[:, halves[parity]] for v in pair]
            rows.append(tripled(jnp.concatenate(parts, axis=1), 1))
        data = jnp.concatenate(rows, axis=0)
        outs.append(jnp.dot(data, right[parity][...], preferred_element_type=F32))
    total, gap = outs[0] + outs[1], outs[0] - outs[1]
    result = []
    for at in range(len(values)):
        rows = slice(at * tall, (at + 1) * tall)
        result.append(
            [jnp.concatenate([total[rows, part], gap[rows, part]], axis=1) for part in halves]
        )
    return result


def neighbours():
    row, column = lax.axis_index("ty"), lax.axis_index("tx")
    has = {
        "up": row > 0,
        "down": row < lax.axis_size("ty") - 1,
        "left": column > 0,
        "right": column < lax.axis_size("tx") - 1,
    }
    where = {
        "up": {"ty": row - 1},
        "down": {"ty": row + 1},
        "left": {"tx": column - 1},
        "right": {"tx": column + 1},
    }
    return has, where


def greet(has, where):
    barrier = pltpu.get_barrier_semaphore()
    for side, there in has.items():

        @pl.when(there)
        def _():
            pl.semaphore_signal(
                barrier, inc=1, device_id=where[side], device_id_type=pl.DeviceIdType.MESH
            )

    peers = sum(there.astype(jnp.int32) for there in has.values())
    pl.semaphore_wait(barrier, peers)


class Links:
    def __init__(self, sems):
        self.sems, self.every = sems, []

    def link(self, source, target, device, sends, receives):
        at = len(self.every)
        made = Link(source, target, self.sems, at, device, sends, receives)
        self.every.append(made)
        return made

    def sent(self, but):
        for made in self.every:
            if made not in but:
                made.sent()


class Link:
    def __init__(self, source, target, sems, at, device, sends, receives):
        self.copy = pltpu.make_async_remote_copy(
            src_ref=source,
            dst_ref=target,
            send_sem=sems[0].at[at],
            recv_sem=sems[1].at[at],
            device_id=device,
            device_id_type=pl.DeviceIdType.MESH,
        )
        self.sends, self.receives = sends, receives

    def start(self):
        pl.when(self.sends)(self.copy.start)

    def sent(self):
        pl.when(self.sends)(self.copy.wait_send)

    def arrived(self):
        pl.when(self.receives)(self.copy.wait_recv)


class Halo:
    def __init__(self, own, regions, links, has, where):
        planes, width = own.shape[0], own.shape[-1]
        forwards = has["up"] & has["right"], has["down"] & has["right"]
        self.has = has
        self.across, self.down, self.corner = {}, {}, {}
        for plane in range(planes):
            for piece, cut in enumerate(HALO_ROWS[plane]):
                rows = rows_of(cut, width)
                mine = own.at[plane, rows]
                right, below, diagonal = [
                    regions[plane // 2].at[plane % 2, quarter, rows] for quarter in (1, 2, 3)
                ]
                key = plane, piece
                self.across[key] = links.link(
                    mine, right, where["left"], has["left"], has["right"]
                )
                self.down[key] = links.link(mine, below, where["up"], has["up"], has["down"])
                self.corner[key] = links.link(right, diagonal, where["up"], *forwards)

    def blank(self, region):
        has = self.has
        zeros = jnp.zeros(region.shape[2:], F32)
        there = has["right"], has["down"], has["down"] & has["right"]
        for plane in range(2):
            for quarter in (1, 2, 3):

                @pl.when(jnp.logical_not(there[quarter - 1]))
                def _():
                    region[plane, quarter] = zeros

    def forward(self, plane, piece):
        self.across[plane, piece].arrived()
        self.corner[plane, piece].start()

    def finish(self, keys):
        for key in keys:
            self.down[key].arrived()
            self.corner[key].arrived()


class Sums:
    def __init__(self, totals, passing, got, links, has, where):
        self.totals, self.passing, self.got, self.has = totals, passing, got, has
        planes, width = passing.shape[0], passing.shape[-1]
        self.corner, self.down, self.across = {}, {}, {}
        for plane in range(planes):
            for piece, cut in enumerate(SUM_ROWS[plane]):
                rows = rows_of(cut, width)
                self.corner[plane, piece] = links.link(
                    totals.at[plane, 3, rows],
                    got.at[0, plane, rows],
                    where["down"],
                    has["down"],
                    has["up"],
                )
                self.across[plane, piece] = links.link(
                    passing.at[plane, rows],
                    got.at[2, plane, rows],
                    where["right"],
                    has["right"],
                    has["left"],
                )
            self.down[plane] = links.link(
                totals.at[plane, 2], got.at[1, plane], where["down"], has["down"], has["up"]
            )

    def start(self, planes, pieces=None):
        last = len(SUM_ROWS[planes[0]]) - 1
        for piece in range(last + 1) if pieces is None else pieces:
            for plane in planes:
                self.corner[plane, piece].start()
            if piece == last:
                for plane in planes:
                    self.down[plane].start()

    def turn(self, planes, pieces=None):
        for piece in range(len(SUM_ROWS[planes[0]])) if pieces is None else pieces:
            for plane in planes:
                rows = rows_of(SUM_ROWS[plane][piece], self.passing.shape[-1])
                self.corner[plane, piece].arrived()
                came = jnp.where(self.has["up"], self.got[0, plane, rows], 0.0)
                self.passing[plane, rows] = self.totals[plane, 1, rows] + came
                self.across[plane, piece].start()

    def finish(self, planes):
        for plane in planes:
            self.down[plane].arrived()
            for piece in range(len(SUM_ROWS[plane])):
                self.across[plane, piece].arrived()

    def came(self, plane):
        above = jnp.where(self.has["up"], self.got[1, plane], 0.0)
        beside = jnp.where(self.has["left"], self.got[2, plane], 0.0)
        return above + beside

    def total(self, plane):
        return self.totals[plane, 0] + self.came(plane)


def turn_of(phase):
    half = phase * 0.5
    square = half * half
    for at in range(7, -1, -1):
        sign = -1.0 if at % 2 else 1.0
        if at == 7:
            cosine, sine = sign * (1.0 / math.factorial(14)), sign * (1.0 / math.factorial(15))
        else:
            cosine = cosine * square + sign / math.factorial(2 * at)
            sine = sine * square + sign / math.factorial(2 * at + 1)
    sine = sine * half
    return 1.0 - 2.0 * sine * sine, 2.0 * sine * cosine


def even_odd(value):
    width = value.shape[0]
    high, low = split(value)
    rest = (value - high.astype(F32) - low.astype(F32)).astype(BF16)
    new = lax.broadcasted_iota(jnp.int32, (width, width), 0)
    old = lax.broadcasted_iota(jnp.int32, (width, width), 1)
    wanted = jnp.where(new < width // 2, 2 * new, 2 * new - width + 1)
    pick = jnp.where(old == wanted, 1.0, 0.0).astype(BF16)
    rows = jnp.dot(pick, jnp.concatenate([high, low, rest], axis=1), preferred_element_type=F32)
    old = lax.broadcasted_iota(jnp.int32, (width, width), 0)
    new = lax.broadcasted_iota(jnp.int32, (width, width), 1)
    wanted = jnp.where(new < width // 2, 2 * new, 2 * new - width + 1)
    pick = jnp.where(old == wanted, 1.0, 0.0).astype(BF16)
    return jnp.dot(
        rows.astype(BF16), jnp.concatenate([pick, pick, pick], axis=0), preferred_element_type=F32
    )


def place(shape, coords, slot, row=0):
    rows = lax.broadcasted_iota(jnp.int32, shape, 0) + row
    columns = lax.broadcasted_iota(jnp.int32, shape, 1)
    return rows >= coords[0, slot], columns >= coords[1, slot]


def window(region, coords, slot, start=0, stop=None):
    width = region.shape[-1]
    stop = stop or width
    at = slice(start, stop)
    rows, columns = place((stop - start, width), coords, slot, start)
    return [
        jnp.where(
            columns,
            jnp.where(rows, region[plane, 0, at], region[plane, 2, at]),
            jnp.where(rows, region[plane, 1, at], region[plane, 3, at]),
        )
        for plane in range(2)
    ]


def deposit(source, totals, first, coords, part=(0, 4)):
    width = totals.shape[-1]
    tall = 32

    first_row, last_row = [width * bound // 4 for bound in part]

    @pl.loop(first_row // tall, last_row // tall)
    def _(piece):
        at = pl.ds(pl.multiple_of(piece * tall, tall), tall)
        sums = None
        for slot in range(coords.shape[1]):
            rows, columns = place((tall, width), coords, slot, piece * tall)
            parts = []
            for value in source(slot, at):
                left, right = jnp.where(columns, value, 0.0), jnp.where(columns, 0.0, value)
                for side, mask in ((left, rows), (right, rows)):
                    parts.append(jnp.where(mask, side, 0.0))
                for side, mask in ((left, rows), (right, rows)):
                    parts.append(jnp.where(mask, 0.0, side))
            sums = parts if sums is None else [a + b for a, b in zip(sums, parts)]
        for index, total in enumerate(sums):
            totals[first + index // 4, index % 4, at] = total


def stage(count, source, between, after, tables, hook):
    forth, back = tables
    spectra = to_spectrum([source(slot) for slot in range(count)], *forth)
    hook(0)
    moved = [between(slot, *pair) for slot, pair in enumerate(spectra)]
    outs = from_spectrum(moved, *back)
    hook(1)
    for slot, pair in enumerate(outs):
        after(slot, *pair)


def kernel(coords, live, own, probe_in, phase_in, amplitude_in, left_in, right_in, *refs):
    out, updated, one, two, twice, phase, amplitude, left_t, right_t, probe, wave, back, *refs = refs
    inverse, totals, passing, got, local, parting, gates, *sems = refs
    width = own.shape[-1]
    count = coords.shape[1]
    has, where = neighbours()
    greet(has, where)
    links = Links(sems)
    halo = Halo(own, (one, two), links, has, where)
    sums = Sums(totals, passing, got, links, has, where)
    row = lax.axis_index("ty")
    even = lax.rem(row, 2) == 0
    odd = jnp.logical_not(even)

    ones = [(plane, piece) for plane in (0, 1) for piece in range(len(HALVES))]
    twos = [[(plane, piece) for plane in (2, 3)] for piece in range(len(HALO_ROWS[2]))]
    all_twos = sum(twos, [])

    def across(keys):
        for key in keys:
            halo.across[key].start()

    def down(keys):
        for key in keys:
            halo.down[key].start()

    def forward(keys):
        for key in keys:
            halo.forward(*key)

    def hand(at, step):
        @pl.when((row + step >= 0) & (row + step < lax.axis_size("ty")))
        def _():
            pl.semaphore_signal(
                gates.at[at],
                inc=1,
                device_id={"ty": row + step},
                device_id_type=pl.DeviceIdType.MESH,
            )

    pl.when(even)(lambda: across(ones))
    down(ones)
    fetches = [
        pltpu.make_async_copy(source, target, local.at[at])
        for at, (source, target) in enumerate(
            [
                (probe_in, twice.at[:, slice(0, width)]),
                (probe_in, twice.at[:, slice(width, 2 * width)]),
                (phase_in, phase.at[0]),
                (amplitude_in, amplitude),
                (left_in, left_t),
                (right_in, right_t),
                (own.at[0:2], one.at[:, 0]),
                (own.at[2:4], two.at[:, 0]),
            ]
        )
    ]
    for fetch in fetches:
        fetch.start()
    for fetch in fetches[:2]:
        fetch.wait()

    @pl.loop(0, count)
    def _(slot):
        top, left = coords[0, slot], coords[1, slot]
        alive = jnp.minimum(jnp.maximum(live[0] - slot, 0), 1).astype(F32)
        start = width - top
        for plane in range(2):
            rows = twice[plane, pl.ds((start >> 3) * 8, width + 8), :]
            rows = pltpu.roll(rows, lax.rem(width + 8 - (start & 7), width + 8), 0)[:width]
            probe[slot, plane] = pltpu.roll(rows, left, 1) * alive

    def power(of):
        def source(slot, rows):
            real, imag = of[slot, 0, rows], of[slot, 1, rows]
            return [real * real + imag * imag]

        return source

    def crossed(of, by):
        def source(slot, rows):
            real, imag = by[slot, 0, rows], by[slot, 1, rows]
            first, second = of[slot, 0, rows], of[slot, 1, rows]
            return [first * real + second * imag, first * imag - second * real]

        return source

    deposit(power(probe), totals, 0, coords)
    sums.start([0])
    halo.blank(one)
    halo.blank(two)

    @pl.when(even)
    def _():
        forward(ones[: len(HALVES)])
        halo.across[1, 0].sent()
        hand(0, 1)
        forward(ones[len(HALVES) :])
        down(all_twos)

    fetches[2].wait()
    cosine, sine = turn_of(phase[0])
    phase[0], phase[1] = even_odd(cosine), even_odd(sine)

    @pl.when(odd)
    def _():
        pl.semaphore_wait(gates.at[0], 1)
        across(ones)

    fetches[3].wait()

    @pl.loop(0, count)
    def _(slot):
        amplitude[slot] = even_odd(amplitude[slot])

    sums.turn([0])
    for fetch in fetches[4:]:
        fetch.wait()

    @pl.when(odd)
    def _():
        forward(ones[: len(HALVES)])
        halo.across[1, 0].sent()
        hand(1, -1)
        forward(ones[len(HALVES) :])
        down(all_twos)

    @pl.when(even)
    def _():
        pl.when(has["down"])(lambda: pl.semaphore_wait(gates.at[1], 1))
        across(all_twos)

    halo.finish(ones)
    forth = [left_t.at[0], left_t.at[1]], [right_t.at[0], right_t.at[1]]
    tables = forth, ([left_t.at[2], left_t.at[3]], [right_t.at[2], right_t.at[3]])

    def first_source(slot):
        real, imag = window(one, coords, slot)
        probe_r, probe_i = probe[slot, 0], probe[slot, 1]
        return probe_r * real - probe_i * imag, probe_r * imag + probe_i * real

    def first_between(slot, real, imag):
        return real * phase[0] - imag * phase[1], real * phase[1] + imag * phase[0]

    def keep(target):
        def after(slot, real, imag):
            target[slot, 0], target[slot, 1] = real, imag

        return after

    def nothing(spot):
        pass

    @pl.when(even)
    def _():
        halo.across[2, 0].sent()
        hand(2, 1)

    @pl.when(odd)
    def _():
        pl.semaphore_wait(gates.at[2], 1)
        across(all_twos)

    def share(spot):
        pl.when(even)(lambda: forward(twos[spot]))

    stage(count, first_source, first_between, keep(wave), tables, share)
    deposit(power(wave), totals, 1, coords)
    sums.start([1])
    pl.when(even)(lambda: forward(twos[2]))
    sums.turn([1])
    half, tall = width // 2, width // 4
    left_f, right_f = tables[0]
    left_b, right_b = tables[1]

    def exits(piece):
        at = rows_of(piece, width)
        values = []
        for slot in range(count):
            second_r, second_i = window(two, coords, slot, at.start, at.stop)
            wave_r, wave_i = [wave[slot, part, at] for part in range(2)]
            values.append(
                (wave_r * second_r - wave_i * second_i, wave_r * second_i + wave_i * second_r)
            )
        return rows_to_spectrum(values, right_f)

    def second_between(slot, real, imag):
        size = jnp.minimum(lax.rsqrt(real * real + imag * imag), 2.0)
        ratio = amplitude[slot] * size - 1.0
        return real * ratio, imag * ratio

    rows, parts = [], []
    for piece, keys in enumerate(twos):
        pl.when(odd)(lambda: forward(keys))
        halo.finish(keys)
        rows.append(exits(HALO_ROWS[2][piece]))
        if piece > 0:
            at = (piece - 1) * tall
            tops = [[v[at : at + tall] for v in pair] for pair in rows[0]]
            depth = slice((piece - 1) * 6 * tall, piece * 6 * tall)
            parts.append(columns_part(tops, rows[piece], left_f, depth))
    far = columns_to_spectrum(*parts, count)
    moved = [second_between(slot, *pair) for slot, pair in enumerate(far)]
    sets = columns_from_spectrum(moved, left_b)
    for piece, cut in enumerate(EARLY):
        at = rows_of(cut, width)
        side = at.start // half
        inside = slice(at.start - side * half, at.stop - side * half)
        values = [[v[inside] for v in pair] for pair in sets[side]]
        for slot, pair in enumerate(rows_from_spectrum(values, right_b)):
            for part in range(2):
                back[slot, part, at] = pair[part]
        deposit(crossed(wave, back), totals, 2, coords, cut)
        sums.start([2, 3], [piece])
        pl.when(jnp.logical_not(has["up"]))(lambda: sums.turn([2, 3], [piece]))
        if piece > 0:
            pl.when(odd)(lambda: sums.turn([2, 3], [piece - 1]))

    def third_source(slot):
        second_r, second_i = window(two, coords, slot)
        real, imag = back[slot, 0], back[slot, 1]
        return second_r * real + second_i * imag, second_r * imag - second_i * real

    def third_between(slot, real, imag):
        return real * phase[0] + imag * phase[1], imag * phase[0] - real * phase[1]

    far = even & has["up"]
    pl.when(odd)(lambda: sums.turn([2, 3], [2]))

    def turn_far(spot):
        pl.when(far)(lambda: sums.turn([2, 3], [[0, 1], [2]][spot]))

    stage(count, third_source, third_between, keep(back), tables, turn_far)
    deposit(crossed(probe, back), totals, 4, coords)
    sums.start([4, 5])
    sums.turn([4, 5])
    sums.finish([0, 1, 2, 3])
    inverse[...] = 1.0 / (sums.total(0) + 1.0)
    leaving = [pltpu.make_async_copy(updated.at[at], out.at[at], parting.at[at]) for at in range(4)]
    for plane in range(2):
        updated[2 + plane] = two[plane, 0] + sums.total(2 + plane) / (sums.total(1) + 1.0)
        leaving[2 + plane].start()
    for plane in range(2):
        updated[plane] = one[plane, 0] + totals[4 + plane, 0] * inverse[...]
    for plane in range(2):
        sums.finish([4 + plane])
        updated[plane] += sums.came(4 + plane) * inverse[...]
        leaving[plane].start()
    pl.when(odd)(halo.across[2, 0].sent)
    for copy in leaving:
        copy.wait()
    links.sent([halo.across[1, 0], halo.across[2, 0]])


def on_device(object_planes, probe, phase, coords, live, amplitude):
    width = probe.shape[-1]
    slots = coords.shape[2]
    left_t, right_t = dft_tables(width)
    smem = pl.BlockSpec(memory_space=pltpu.SMEM)
    hbm = pl.BlockSpec(memory_space=pltpu.HBM)

    def scratch(*shape):
        return pltpu.VMEM((*shape, width, width), F32)

    links = sum(3 * len(cuts) for cuts in HALO_ROWS)
    links += sum(2 * len(cuts) + 1 for cuts in SUM_ROWS)

    return pl.pallas_call(
        kernel,
        out_shape=jax.ShapeDtypeStruct(object_planes.shape, F32),
        in_specs=[smem] * 2 + [hbm] * 6,
        out_specs=hbm,
        scratch_shapes=[
            scratch(4),
            scratch(2, 4),
            scratch(2, 4),
            pltpu.VMEM((2, 2 * width + 8, width), F32),
            scratch(2),
            scratch(slots),
            pltpu.VMEM(left_t.shape, BF16),
            pltpu.VMEM(right_t.shape, BF16),
            scratch(slots, 2),
            scratch(slots, 2),
            scratch(slots, 2),
            scratch(),
            scratch(6, 4),
            scratch(6),
            scratch(3, 6),
            pltpu.SemaphoreType.DMA((8,)),
            pltpu.SemaphoreType.DMA((4,)),
            pltpu.SemaphoreType.REGULAR((3,)),
            pltpu.SemaphoreType.DMA((links,)),
            pltpu.SemaphoreType.DMA((links,)),
        ],
        compiler_params=pltpu.CompilerParams(
            vmem_limit_bytes=60 << 20, collective_id=0, has_side_effects=True
        ),
        cost_estimate=pl.CostEstimate(
            flops=48 * slots * width**3, bytes_accessed=8 << 20, transcendentals=0
        ),
        name="iteration",
    )(coords[0, 0].T, live[0], object_planes, probe, phase, amplitude[0, 0], left_t, right_t)


def solution(mesh):
    return jax.shard_map(
        on_device,
        mesh=mesh,
        in_specs=(
            P(None, ("groups", "ty"), "tx"),
            P(),
            P(),
            P(("groups", "ty"), "tx", None, None),
            P(("groups", "ty"), "tx"),
            P(("groups", "ty"), "tx", None, None, None),
        ),
        out_specs=P(None, ("groups", "ty"), "tx"),
        check_vma=False,
    )
```
